128 devices in a mesh: section: 8 (over x_hi, y), dp: 16 (over z, x_lo, core).
Axes of the slice: x: 4 (x_hi: 2, x_lo: 2; x = x_hi * 2 + x_lo), y: 4, z: 4, core: 2. Of those that a mesh axis runs over, the one named last changes fastest.
Arguments:
- section_inputs: bfloat16 [2, 8, 4, 2048, 1024], P(None, 'section', None, 'dp'), may hold values from -6 to 6
- top_grad: bfloat16 [2, 4, 2048, 1024], P(None, None, 'dp'), may hold values from -0.125 to 0.125
- plan: int32 [2, 4], replicated, may hold values from 0 to 3, each once within a row
- up_weight: bfloat16 [2, 8, 1024, 2048], P(None, 'section'), as said below
- down_weight: bfloat16 [2, 8, 2048, 1024], P(None, 'section'), as said below
- up_moment: float32 [8, 1024, 2048], P('section', 'dp'), may hold values from -6 to 6
- down_moment: float32 [8, 2048, 1024], P('section', 'dp'), may hold values from -6 to 6
Outputs:
- new_up_weight: bfloat16 [2, 8, 1024, 2048], P(None, 'section', 'dp')
- new_down_weight: bfloat16 [2, 8, 2048, 1024], P(None, 'section', 'dp')
- new_up_moment: float32 [8, 1024, 2048], P('section', 'dp')
- new_down_moment: float32 [8, 2048, 1024], P('section', 'dp')
The draws below stay inside these ranges and needn't reach their ends.
Inputs may be any that keep to these rules, and one draw needn't show every extreme that they name: up_weight[1, s] equals up_weight[0, 7 - s] for every s: both relays hold the same model. down_weight[1, s] equals down_weight[0, 7 - s] for every s. `plan`: each row names every micro-batch once.
All inputs are finite; a program needn't handle non-finite values.
Results may differ from the reference program's by a relative error of at most 0.02.
Values may be sent and summed in bfloat16 or wider, within the bound.
A program may use at most 128 MiB of HBM per device.

```python
import jax
import jax.numpy as jnp
from jax import lax

D = 1024
FF_WIN = 2048
MB = 4
TOK_MB = 128
SECTIONS = 8
TOKENS = 2048
N_DP = 16


def draw_up_weight(key, part):
    inner = jax.random.fold_in(key, 11)
    base = jax.random.normal(inner, (SECTIONS, D, FF_WIN), jnp.float32) * D ** (-0.5)
    return jnp.stack([base, base[::-1]]).astype(jnp.bfloat16)


def draw_down_weight(key, part):
    inner = jax.random.fold_in(key, 23)
    base = jax.random.normal(inner, (SECTIONS, FF_WIN, D), jnp.float32) * FF_WIN ** (-0.5)
    return jnp.stack([base, base[::-1]]).astype(jnp.bfloat16)


def steps_of(rng, dims, cuts, smallest, largest):
    loudness, own = 1.0, jax.random.fold_in(rng, 6)
    for position, shards_of in cuts:
        steps = jnp.exp(jax.random.uniform(jax.random.fold_in(own, position), (shards_of,), jnp.float32, smallest / len(cuts), largest / len(cuts)))
        loudness = loudness * jnp.repeat(steps, dims[position] // shards_of).reshape([-1 if axis == position else 1 for axis in range(len(dims))])
    return loudness


def bell_draw(stream_key, extent, width, most, cuts=(), held_as=jnp.bfloat16):
    loudness = steps_of(stream_key, extent, cuts, -0.22, 0.18) if cuts else 1.0
    result = jax.random.normal(stream_key, extent, jnp.float32) * width * loudness
    return jnp.minimum(jnp.maximum(result, -most), most).astype(held_as)


def setup_inputs(seed: int = 0) -> dict:
    key_of = jax.random.split(jax.random.key(seed), 8)
    return {
        "section_inputs": bell_draw(key_of[0], (2, SECTIONS, MB, TOKENS, D), 1.0, 6.0, ((1, 8), (3, 16))),
        "top_grad": bell_draw(key_of[1], (2, MB, TOKENS, D), ((2 * N_DP * MB * TOK_MB) ** -0.5), 0.125, ((2, 16),)),
        "plan": jax.vmap(lambda own: jax.random.permutation(own, MB))(jax.random.split(key_of[2], 2)).reshape((2, MB)).astype(jnp.int32),
        "up_weight": draw_up_weight(jax.random.fold_in(key_of[7], 71), 0),
        "down_weight": draw_down_weight(jax.random.fold_in(key_of[7], 71), 0),
        "up_moment": bell_draw(key_of[5], (SECTIONS, D, FF_WIN), 1.0, 6.0, ((0, 8), (1, 16)), jnp.float32),
        "down_moment": bell_draw(key_of[6], (SECTIONS, FF_WIN, D), 1.0, 6.0, ((0, 8), (1, 16)), jnp.float32),
    }


norm_epsilon = 1e-06
momentum_decay = 0.9
step_size = 0.01
root_half = 0.7071067811865476
inv_root_tau = 0.3989422804014327

def gelu_value(preact):
    return 0.5 * preact * (1.0 + lax.erf(preact * root_half))

def gelu_slope(preact):
    return 0.5 * (1.0 + lax.erf(preact * root_half)) + preact * jnp.exp(-0.5 * preact * preact) * inv_root_tau

def times_transpose(left, right):
    return lax.dot_general(left, right, (((1,), (1,)), ((), ())), preferred_element_type=jnp.float32)

def local_backward(inputs, incoming, w_up, w_down):
    preact = jnp.dot(inputs, w_up, preferred_element_type=jnp.float32)
    hidden = gelu_value(preact).astype(jnp.bfloat16)
    summed = inputs.astype(jnp.float32) + jnp.dot(hidden, w_down, preferred_element_type=jnp.float32)
    centre = summed - lax.optimization_barrier(jnp.mean(summed, axis=-1, keepdims=True))
    scale_inv = lax.rsqrt(lax.optimization_barrier(jnp.mean(centre * centre, axis=-1, keepdims=True)) + norm_epsilon)
    normed = centre * scale_inv
    upstream = incoming.astype(jnp.float32)
    grad_sum = scale_inv * (upstream - lax.optimization_barrier(jnp.mean(upstream, axis=-1, keepdims=True)) - normed * lax.optimization_barrier(jnp.mean(upstream * normed, axis=-1, keepdims=True)))
    grad_sum_low = grad_sum.astype(jnp.bfloat16)
    grad_pre = (times_transpose(grad_sum_low, w_down) * gelu_slope(preact)).astype(jnp.bfloat16)
    grad_in = (grad_sum + times_transpose(grad_pre, w_up)).astype(jnp.bfloat16)
    return (grad_in, hidden, grad_pre, grad_sum_low)

def group_partial(left, right):
    left_groups = left.reshape(MB, N_DP, TOK_MB, left.shape[-1]).astype(jnp.float32)
    right_groups = right.reshape(MB, N_DP, TOK_MB, right.shape[-1]).astype(jnp.float32)
    parts = jnp.einsum('mgtd,mgtf->gdf', left_groups, right_groups)
    rounded = lax.optimization_barrier(parts.astype(jnp.bfloat16))
    return lax.optimization_barrier(jnp.sum(rounded.astype(jnp.float32), axis=0))

def section_backward(inputs, incoming, w_up, w_down):
    flat_in = inputs.reshape(MB * TOKENS, D)
    flat_grad = incoming.reshape(MB * TOKENS, D)
    grad_in, hidden, grad_pre, grad_sum_low = local_backward(flat_in, flat_grad, w_up, w_down)
    up_part = group_partial(flat_in, grad_pre)
    down_part = group_partial(hidden, grad_sum_low)
    return (grad_in.reshape(MB, TOKENS, D), up_part, down_part)

def reference(section_inputs, top_grad, plan, up_weight, down_weight, up_moment, down_moment):
    up_sums = [[None] * SECTIONS, [None] * SECTIONS]
    down_sums = [[None] * SECTIONS, [None] * SECTIONS]
    for direction in range(2):
        if direction == 0:
            devices = list(range(SECTIONS - 1, -1, -1))
        else:
            devices = list(range(SECTIONS))
        incoming = top_grad[direction]
        order = plan[direction].astype(jnp.int32)
        for device in devices:
            inputs = jnp.take(section_inputs[direction, device], order, axis=0)
            incoming, up_part, down_part = section_backward(inputs, incoming, up_weight[direction, device], down_weight[direction, device])
            up_sums[direction][device] = up_part
            down_sums[direction][device] = down_part
    grad_up = jnp.stack([up_sums[0][k] + up_sums[1][SECTIONS - 1 - k] for k in range(SECTIONS)])
    grad_down = jnp.stack([down_sums[0][k] + down_sums[1][SECTIONS - 1 - k] for k in range(SECTIONS)])
    new_up_moment = momentum_decay * up_moment + grad_up
    new_down_moment = momentum_decay * down_moment + grad_down
    fresh_up = (up_weight[0].astype(jnp.float32) - step_size * new_up_moment).astype(jnp.bfloat16)
    fresh_down = (down_weight[0].astype(jnp.float32) - step_size * new_down_moment).astype(jnp.bfloat16)
    new_up_weight = jnp.stack([fresh_up, fresh_up[::-1]])
    new_down_weight = jnp.stack([fresh_down, fresh_down[::-1]])
    return (new_up_weight, new_down_weight, new_up_moment, new_down_moment)
```

```python
import functools

import jax
import jax.numpy as jnp
from jax import lax
from jax.experimental import pallas as pl
from jax.experimental.pallas import tpu as pltpu
from jax.sharding import PartitionSpec as P

norm_epsilon = 1e-06
momentum_decay = 0.9
step_size = 0.01
root_half = 0.7071067811865476
inv_root_tau = 0.3989422804014327
MESH = pl.DeviceIdType.MESH
bf16 = jnp.bfloat16
f32 = jnp.float32


def times_transpose(left, right):
    return lax.dot_general(
        left, right, (((1,), (1,)), ((), ())), preferred_element_type=f32
    )


def contract_rows(left, right):
    return lax.dot_general(
        left, right, (((0,), (0,)), ((), ())), preferred_element_type=f32
    )


def relay_kernel(
    sections, micro, rows, model, width, tile, ahead,
    inputs_hbm, top_hbm, up_hbm, down_hbm,
    up_out, down_out,
    w_up, w_down, x_buf, hidden, slope, normed, scale_buf, grad_pre, grad_low, e_buf, sent,
    w_sem, own_sem, swap_send, swap_recv, top_send, e_recv, e_send,
):
    section = lax.axis_index("section")
    replica = lax.axis_index("dp")
    core = lax.rem(replica, 2)
    other = replica + 1 - 2 * core
    position = jnp.where(core == 0, sections - 1 - section, section)
    step_to = 2 * core - 1
    after = lax.rem(section + step_to + sections, sections)
    before = lax.rem(section - step_to + sections, sections)
    chunks = 2 * micro
    last = sections - 1

    w_up_copy = pltpu.make_async_copy(up_hbm.at[core, 0], w_up, w_sem.at[0])
    w_down_copy = pltpu.make_async_copy(down_hbm.at[core, 0], w_down, w_sem.at[1])

    def own_copy(slot):
        return pltpu.make_async_copy(
            inputs_hbm.at[core, slot], x_buf.at[2 * slot + core], own_sem.at[slot]
        )

    def swap_copy(slot):
        return pltpu.make_async_remote_copy(
            src_ref=inputs_hbm.at[1 - core, slot],
            dst_ref=x_buf.at[2 * slot + core],
            send_sem=swap_send.at[slot],
            recv_sem=swap_recv.at[slot],
            device_id=(section, other),
            device_id_type=MESH,
        )

    def top_own(slot):
        return pltpu.make_async_copy(
            top_hbm.at[core, slot], e_buf.at[2 * slot + core], e_recv.at[2 * slot + core]
        )

    def top_swap(slot):
        return pltpu.make_async_remote_copy(
            src_ref=top_hbm.at[1 - core, slot],
            dst_ref=e_buf.at[2 * slot + core],
            send_sem=top_send.at[slot],
            recv_sem=e_recv.at[2 * slot + core],
            device_id=(section, other),
            device_id_type=MESH,
        )

    def relay_copy(chunk):
        return pltpu.make_async_remote_copy(
            src_ref=sent.at[chunk],
            dst_ref=e_buf.at[chunk],
            send_sem=e_send.at[chunk],
            recv_sem=e_recv.at[chunk],
            device_id=(after, replica),
            device_id_type=MESH,
        )

    w_up_copy.start()
    for slot in range(micro):
        own_copy(slot).start()
    w_down_copy.start()

    barrier = pltpu.get_barrier_semaphore()
    pl.semaphore_signal(barrier, inc=1, device_id=(after, replica), device_id_type=MESH)
    pl.semaphore_signal(barrier, inc=1, device_id=(before, replica), device_id_type=MESH)
    pl.semaphore_signal(barrier, inc=1, device_id=(section, other), device_id_type=MESH)
    pl.semaphore_wait(barrier, 3)

    @pl.when(position == last)
    def _():
        for slot in range(micro):
            top_swap(slot).start()

    for slot in range(micro):
        swap_copy(slot).start()

    @pl.when(position == 0)
    def _():
        for slot in range(micro):
            top_own(slot).start()

    w_up_copy.wait()
    for slot in range(micro):
        own_copy(slot).wait()
        swap_copy(slot).wait()
    w_down_copy.wait()

    def forward(chunk):
        x = x_buf[chunk]

        for n in range(width // tile):
            cols = pl.ds(n * tile, tile)
            preact = jnp.dot(x, w_up[:, cols], preferred_element_type=f32)
            cdf = 0.5 * (1.0 + lax.erf(preact * root_half))
            hidden[chunk, :, cols] = (preact * cdf).astype(bf16)
            slope[chunk, :, cols] = cdf + preact * jnp.exp(-0.5 * preact * preact) * inv_root_tau
        summed = x.astype(f32) + jnp.dot(hidden[chunk], w_down[...], preferred_element_type=f32)
        centre = summed - jnp.mean(summed, axis=-1, keepdims=True)
        scale_inv = lax.rsqrt(jnp.mean(centre * centre, axis=-1, keepdims=True) + norm_epsilon)
        normed[chunk] = centre * scale_inv
        scale_buf[chunk] = jnp.broadcast_to(scale_inv, (rows, 128))

    def backward(chunk):
        pltpu.make_async_copy(sent.at[chunk], e_buf.at[chunk], e_recv.at[chunk]).wait()
        upstream = e_buf[chunk].astype(f32)
        y = normed[chunk]
        scale_inv = scale_buf[chunk][:, :1]
        grad_sum = scale_inv * (
            upstream
            - jnp.mean(upstream, axis=-1, keepdims=True)
            - y * jnp.mean(upstream * y, axis=-1, keepdims=True)
        )
        low = grad_sum.astype(bf16)
        grad_low[pl.ds(pl.multiple_of(chunk * rows, rows), rows), :] = low
        place = pl.ds(pl.multiple_of(chunk * rows, rows), rows)
        for n in range(width // tile):
            cols = pl.ds(n * tile, tile)
            grad = times_transpose(low, w_down[cols, :]) * slope[chunk, :, cols]
            grad_pre[place, cols] = grad.astype(bf16)

        @pl.when(position < last)
        def _():
            sent[chunk] = (grad_sum + times_transpose(grad_pre[place, :], w_up[...])).astype(bf16)
            relay_copy(chunk).start()

    lead = jnp.minimum(chunks, ahead * position)

    @pl.loop(0, 2 * chunks)
    def _(step):
        @pl.when(step < chunks)
        def _():
            forward(step)

        back = step - lead

        @pl.when(jnp.logical_and(back >= 0, back < chunks))
        def _():
            backward(back)

    total = chunks * rows
    span = 256 if model % 256 == 0 else 128

    @pl.loop(0, model // span)
    def _(t):
        cols = pl.ds(pl.multiple_of(t * span, span), span)
        left = x_buf[:, :, cols].reshape(total, span)
        up_out[cols, :] = contract_rows(left, grad_pre[...]).astype(bf16)

    @pl.loop(0, width // span)
    def _(t):
        cols = pl.ds(pl.multiple_of(t * span, span), span)
        left = hidden[:, :, cols].reshape(total, span)
        down_out[cols, :] = contract_rows(left, grad_low[...]).astype(bf16)

    @pl.when(position < last)
    def _():
        for chunk in range(chunks):
            relay_copy(chunk).wait_send()

    @pl.when(position == last)
    def _():
        for slot in range(micro):
            top_swap(slot).wait_send()


def relay(sections, ordered, top_grad, up_weight, down_weight):
    micro, rows, model = ordered.shape[1:]
    width = up_weight.shape[3]
    chunks = 2 * micro
    total = chunks * rows
    dma = pltpu.SemaphoreType.DMA
    flops = 2 * 6 * total * model * width
    return pl.pallas_call(
        functools.partial(relay_kernel, sections, micro, rows, model, width, min(512, width), 3),
        out_shape=[
            jax.ShapeDtypeStruct((model, width), bf16),
            jax.ShapeDtypeStruct((width, model), bf16),
        ],
        in_specs=[pl.BlockSpec(memory_space=pl.ANY)] * 4,
        out_specs=[pl.BlockSpec(memory_space=pltpu.VMEM)] * 2,
        scratch_shapes=[
            pltpu.VMEM((model, width), bf16),
            pltpu.VMEM((width, model), bf16),
            pltpu.VMEM((chunks, rows, model), bf16),
            pltpu.VMEM((chunks, rows, width), bf16),
            pltpu.VMEM((chunks, rows, width), f32),
            pltpu.VMEM((chunks, rows, model), f32),
            pltpu.VMEM((chunks, rows, 128), f32),
            pltpu.VMEM((total, width), bf16),
            pltpu.VMEM((total, model), bf16),
            pltpu.VMEM((chunks, rows, model), bf16),
            pltpu.VMEM((chunks, rows, model), bf16),
            dma((2,)),
            dma((micro,)),
            dma((micro,)),
            dma((micro,)),
            dma((micro,)),
            dma((chunks,)),
            dma((chunks,)),
        ],
        compiler_params=pltpu.CompilerParams(
            collective_id=0, has_side_effects=True, vmem_limit_bytes=60 * 1024 * 1024
        ),
        cost_estimate=pl.CostEstimate(flops=flops, bytes_accessed=24 << 20, transcendentals=0),
    )(ordered, top_grad, up_weight, down_weight)


def on_device(section_inputs, top_grad, plan, up_weight, down_weight, up_moment, down_moment):
    sections = lax.axis_size("section")
    replicas = lax.axis_size("dp")
    replica = lax.axis_index("dp")
    core = lax.rem(replica, 2)
    mirror = [(i, sections - 1 - i) for i in range(sections)]
    swap = [(i, i ^ 1) for i in range(replicas)]
    their_moment_up = lax.ppermute(up_moment[0].astype(bf16), "section", mirror)
    their_moment_down = lax.ppermute(down_moment[0].astype(bf16), "section", mirror)
    ordered = jnp.stack([section_inputs[c, 0][plan[c]] for c in range(2)])
    part_up, part_down = relay(sections, ordered, top_grad, up_weight, down_weight)
    groups = [list(range(0, replicas, 2)), list(range(1, replicas, 2))]

    def reduced(part):
        held = lax.psum_scatter(
            part, "dp", scatter_dimension=0, axis_index_groups=groups, tiled=True
        )
        half = held.shape[0] // 2
        mine = lax.dynamic_slice_in_dim(held, core * half, half, 0)
        give = lax.dynamic_slice_in_dim(held, (1 - core) * half, half, 0)
        got = lax.ppermute(give, "dp", swap)
        return jnp.where(core == 0, mine, got), jnp.where(core == 0, got, mine)

    own_up, far_up = reduced(part_up)
    own_down, far_down = reduced(part_down)
    their = [lax.ppermute(v, "section", mirror) for v in (own_up, far_up, own_down, far_down)]
    their_own_up, their_far_up, their_own_down, their_far_down = their

    def update(moment, their_moment, own, far, their_own, their_far, weights):
        rows = moment.shape[0]
        held = lax.dynamic_slice_in_dim(weights[:, 0], replica * rows, rows, 1).astype(f32)
        new = momentum_decay * moment + (own.astype(f32) + their_far.astype(f32))
        fresh = (held[0] - step_size * new).astype(bf16)
        mirrored = momentum_decay * their_moment.astype(f32) + (
            their_own.astype(f32) + far.astype(f32)
        )
        mirror_fresh = (held[1] - step_size * mirrored).astype(bf16)
        return new, jnp.stack([fresh, mirror_fresh])[:, None]

    moment_up, new_up = update(
        up_moment[0], their_moment_up, own_up, far_up, their_own_up, their_far_up, up_weight
    )
    moment_down, new_down = update(
        down_moment[0], their_moment_down, own_down, far_down,
        their_own_down, their_far_down, down_weight,
    )
    return (new_up, new_down, moment_up[None], moment_down[None])


def solution(mesh):
    in_specs = (
        P(None, "section", None, "dp", None),
        P(None, None, "dp", None),
        P(),
        P(None, "section", None, None),
        P(None, "section", None, None),
        P("section", "dp", None),
        P("section", "dp", None),
    )
    out_specs = (
        P(None, "section", "dp", None),
        P(None, "section", "dp", None),
        P("section", "dp", None),
        P("section", "dp", None),
    )
    return jax.shard_map(
        on_device, mesh=mesh, in_specs=in_specs, out_specs=out_specs, check_vma=False
    )
```

```python
import functools

import jax
import jax.numpy as jnp
from jax import lax
from jax.experimental import pallas as pl
from jax.experimental.pallas import tpu as pltpu
from jax.sharding import PartitionSpec as P

norm_epsilon = 1e-06
momentum_decay = 0.9
step_size = 0.01
root_half = 0.7071067811865476
inv_root_tau = 0.3989422804014327
MESH = pl.DeviceIdType.MESH
bf16 = jnp.bfloat16
f32 = jnp.float32


def times_transpose(left, right):
    return lax.dot_general(
        left, right, (((1,), (1,)), ((), ())), preferred_element_type=f32
    )


def contract_rows(left, right):
    return lax.dot_general(
        left, right, (((0,), (0,)), ((), ())), preferred_element_type=f32
    )


def relay_kernel(
    sections, replicas, micro, rows, model, width, tile, ahead,
    inputs_hbm, top_hbm, up_hbm, down_hbm, moment_up_hbm, moment_down_hbm,
    new_up, new_down, new_moment_up, new_moment_down,
    w_up, w_down, x_buf, hidden, slope, normed, scale_buf, grad_pre, grad_low, e_buf, sent,
    part_up, part_down, ring_up, ring_down, pair_up, pair_down, swap_up, swap_down,
    far_up, far_down, moment_up, moment_down, low_up, low_down, their_up, their_down,
    held_up, held_down,
    w_sem, own_sem, swap_send, swap_recv, top_send, e_recv, e_send,
    state_sem, moment_send, moment_recv, ring_send, ring_recv, pair_send, pair_recv,
    give_send, give_recv,
):
    section = lax.axis_index("section")
    replica = lax.axis_index("dp")
    core = lax.rem(replica, 2)
    other = replica + 1 - 2 * core
    side = lax.rem(replica // 2, 2)
    layer = replica // 4
    layers = replicas // 4
    above = lax.rem(replica + 4, replicas)
    below = lax.rem(replica + replicas - 4, replicas)
    beside = replica + 2 - 4 * side
    mirror = sections - 1 - section
    position = jnp.where(core == 0, sections - 1 - section, section)
    step_to = 2 * core - 1
    after = lax.rem(section + step_to + sections, sections)
    before = lax.rem(section - step_to + sections, sections)
    chunks = 2 * micro
    last = sections - 1
    parts = (part_up, part_down)
    rings = (ring_up, ring_down)
    pairs = (pair_up, pair_down)
    swaps = (swap_up, swap_down)
    fars = (far_up, far_down)
    lows = (low_up, low_down)
    theirs = (their_up, their_down)
    moments = (moment_up, moment_down)
    helds = (held_up, held_down)
    halves = (model // (2 * layers), width // (2 * layers))

    w_up_copy = pltpu.make_async_copy(up_hbm.at[core, 0], w_up, w_sem.at[0])
    w_down_copy = pltpu.make_async_copy(down_hbm.at[core, 0], w_down, w_sem.at[1])

    def aligned(start, size):
        return pl.ds(pl.multiple_of(start, size), size)

    def own_copy(slot):
        return pltpu.make_async_copy(
            inputs_hbm.at[core, slot], x_buf.at[2 * slot + core], own_sem.at[slot]
        )

    def remote(src, dst, send, recv, device):
        return pltpu.make_async_remote_copy(
            src_ref=src, dst_ref=dst, send_sem=send, recv_sem=recv,
            device_id=device, device_id_type=MESH,
        )

    def swap_copy(slot):
        return remote(
            inputs_hbm.at[1 - core, slot], x_buf.at[2 * slot + core],
            swap_send.at[slot], swap_recv.at[slot], (section, other),
        )

    def top_own(slot):
        return pltpu.make_async_copy(
            top_hbm.at[core, slot], e_buf.at[2 * slot + core], e_recv.at[2 * slot + core]
        )

    def top_swap(slot):
        return remote(
            top_hbm.at[1 - core, slot], e_buf.at[2 * slot + core],
            top_send.at[slot], e_recv.at[2 * slot + core], (section, other),
        )

    def relay_copy(chunk):
        return remote(
            sent.at[chunk], e_buf.at[chunk], e_send.at[chunk], e_recv.at[chunk], (after, replica)
        )

    def moment_copy(kind):
        return remote(
            lows[kind], theirs[kind], moment_send.at[kind], moment_recv.at[kind], (mirror, replica)
        )

    def ring_block(way, step):
        shift = layers - 1 - step if way == 0 else 1 + step
        return lax.rem(layer + shift, layers)

    def ring_copy(kind, way, step):
        half = halves[kind]
        start = ring_block(way, step) * 2 * half + way * half
        return remote(
            parts[kind].at[aligned(start, half), :], rings[kind].at[way, step],
            ring_send.at[kind, way, step], ring_recv.at[kind, way, step],
            (section, above if way == 0 else below),
        )

    def pair_copy(kind):
        half = halves[kind]
        start = layer * 2 * half + (1 - side) * half
        return remote(
            parts[kind].at[aligned(start, half), :], pairs[kind],
            pair_send.at[kind], pair_recv.at[kind], (section, beside),
        )

    def final_rows(kind, which):
        half = halves[kind]
        quarter = half // 2
        return aligned(layer * 2 * half + side * half + which * quarter, quarter)

    def give_copies(kind):
        return (
            remote(
                parts[kind].at[final_rows(kind, core), :], fars[kind].at[0],
                give_send.at[kind, 0], give_recv.at[kind, 0], (mirror, replica),
            ),
            remote(
                parts[kind].at[final_rows(kind, 1 - core), :], fars[kind].at[1],
                give_send.at[kind, 1], give_recv.at[kind, 1], (mirror, other),
            ),
            remote(
                parts[kind].at[final_rows(kind, 1 - core), :], swaps[kind],
                give_send.at[kind, 2], give_recv.at[kind, 2], (section, other),
            ),
        )

    state_copies = []
    for kind, (held_hbm, moment_hbm) in enumerate(
        ((up_hbm, moment_up_hbm), (down_hbm, moment_down_hbm))
    ):
        state_copies.append(
            pltpu.make_async_copy(moment_hbm.at[0], moments[kind], state_sem.at[kind, 0])
        )
        count = helds[kind].shape[1]
        for c in range(2):
            state_copies.append(
                pltpu.make_async_copy(
                    held_hbm.at[c, 0, aligned(replica * count, count), :],
                    helds[kind].at[c], state_sem.at[kind, 1 + c],
                )
            )

    w_up_copy.start()
    for slot in range(micro):
        own_copy(slot).start()
    w_down_copy.start()
    for copy in state_copies:
        copy.start()

    barrier = pltpu.get_barrier_semaphore()
    for device in (
        (after, replica), (before, replica), (section, other), (section, above),
        (section, below), (section, beside), (mirror, replica), (mirror, other),
    ):
        pl.semaphore_signal(barrier, inc=1, device_id=device, device_id_type=MESH)
    pl.semaphore_wait(barrier, 8)

    @pl.when(position == last)
    def _():
        for slot in range(micro):
            top_swap(slot).start()

    for slot in range(micro):
        swap_copy(slot).start()

    @pl.when(position == 0)
    def _():
        for slot in range(micro):
            top_own(slot).start()

    w_up_copy.wait()
    for slot in range(micro):
        own_copy(slot).wait()
        swap_copy(slot).wait()
    w_down_copy.wait()

    def forward(chunk):
        x = x_buf[chunk]

        for n in range(width // tile):
            cols = pl.ds(n * tile, tile)
            preact = jnp.dot(x, w_up[:, cols], preferred_element_type=f32)
            cdf = 0.5 * (1.0 + lax.erf(preact * root_half))
            hidden[chunk, :, cols] = (preact * cdf).astype(bf16)
            grown = cdf + preact * jnp.exp(-0.5 * preact * preact) * inv_root_tau
            slope[chunk, :, cols] = grown.astype(bf16)
        summed = x.astype(f32) + jnp.dot(hidden[chunk], w_down[...], preferred_element_type=f32)
        centre = summed - jnp.mean(summed, axis=-1, keepdims=True)
        scale_inv = lax.rsqrt(jnp.mean(centre * centre, axis=-1, keepdims=True) + norm_epsilon)
        normed[chunk] = centre * scale_inv
        scale_buf[chunk] = jnp.broadcast_to(scale_inv, (rows, 128))

    def backward(chunk):
        pltpu.make_async_copy(sent.at[chunk], e_buf.at[chunk], e_recv.at[chunk]).wait()
        upstream = e_buf[chunk].astype(f32)
        y = normed[chunk]
        scale_inv = scale_buf[chunk][:, :1]
        grad_sum = scale_inv * (
            upstream
            - jnp.mean(upstream, axis=-1, keepdims=True)
            - y * jnp.mean(upstream * y, axis=-1, keepdims=True)
        )
        low = grad_sum.astype(bf16)
        place = aligned(chunk * rows, rows)
        grad_low[place, :] = low
        for n in range(width // tile):
            cols = pl.ds(n * tile, tile)
            grad = times_transpose(low, w_down[cols, :]) * slope[chunk, :, cols].astype(f32)
            grad_pre[place, cols] = grad.astype(bf16)

        @pl.when(position < last)
        def _():
            sent[chunk] = (grad_sum + times_transpose(grad_pre[place, :], w_up[...])).astype(bf16)
            relay_copy(chunk).start()

    lead = jnp.minimum(chunks, ahead * position)

    @pl.loop(0, 2 * chunks)
    def _(step):
        @pl.when(step < chunks)
        def _():
            forward(step)

        back = step - lead

        @pl.when(jnp.logical_and(back >= 0, back < chunks))
        def _():
            backward(back)

        @pl.when(step == chunks - 1)
        def _():
            for copy in state_copies:
                copy.wait()
            for kind in range(2):
                lows[kind][...] = moments[kind][...].astype(bf16)
                moment_copy(kind).start()

    total = chunks * rows
    span = min(256, 2 * halves[0])

    def up_block(block):
        @pl.loop(0, 2 * halves[0] // span)
        def _(t):
            cols = aligned(block * 2 * halves[0] + t * span, span)
            left = x_buf[:, :, cols].reshape(total, span)
            part_up[cols, :] = contract_rows(left, grad_pre[...]).astype(bf16)

    def down_block(block):
        @pl.loop(0, 2 * halves[1] // span)
        def _(t):
            cols = aligned(block * 2 * halves[1] + t * span, span)
            left = hidden[:, :, cols].reshape(total, span)
            part_down[cols, :] = contract_rows(left, grad_low[...]).astype(bf16)

    def blocks(fill, shifts):
        @pl.loop(0, len(shifts))
        def _(i):
            shift = jnp.where(i == 0, shifts[0], shifts[-1])
            fill(lax.rem(layer + shift, layers))

    def first(kind, fill):
        fill(ring_block(0, 0))
        ring_copy(kind, 0, 0).start()
        fill(ring_block(1, 0))
        ring_copy(kind, 1, 0).start()

    def add_rows(kind, start, size, value):
        place = aligned(start, size)
        held = parts[kind][place, :].astype(f32) + value.astype(f32)
        parts[kind][place, :] = held.astype(bf16)

    def turn(kind, step):
        for way in range(2):
            ring_copy(kind, way, step).wait_recv()
            half = halves[kind]
            start = ring_block(way, step + 1) * 2 * half + way * half
            add_rows(kind, start, half, rings[kind][way, step])
            if step < layers - 2:
                ring_copy(kind, way, step + 1).start()

    def settle(kind):
        half = halves[kind]
        pair_copy(kind).start()
        pair_copy(kind).wait_recv()
        add_rows(kind, layer * 2 * half + side * half, half, pairs[kind][...])
        for copy in give_copies(kind):
            copy.start()

    rest = [2, 0]
    first(0, up_block)
    blocks(up_block, rest)
    first(1, down_block)
    turn(0, 0)
    blocks(down_block, rest)
    turn(1, 0)
    for step in range(1, layers - 2):
        turn(0, step)
        turn(1, step)
    turn(0, layers - 2)
    settle(0)
    turn(1, layers - 2)
    settle(1)

    for kind in range(2):
        moment_copy(kind).wait()

    for kind, (out, out_moment) in enumerate(
        ((new_up, new_moment_up), (new_down, new_moment_down))
    ):
        for copy in give_copies(kind):
            copy.wait_recv()
        own = parts[kind][final_rows(kind, core), :].astype(f32)
        got = swaps[kind][...].astype(f32)
        same = fars[kind][0].astype(f32)
        cross = fars[kind][1].astype(f32)
        zero = core == 0
        grad = jnp.where(zero, own + cross, got + same)
        grad_mirror = jnp.where(zero, got + same, own + cross)
        moment = momentum_decay * moments[kind][...] + grad
        out_moment[...] = moment
        out[0] = (helds[kind][0].astype(f32) - step_size * moment).astype(bf16)
        mirrored = momentum_decay * theirs[kind][...].astype(f32) + grad_mirror
        out[1] = (helds[kind][1].astype(f32) - step_size * mirrored).astype(bf16)

    for kind in range(2):
        for way in range(2):
            for step in range(layers - 1):
                ring_copy(kind, way, step).wait_send()
        pair_copy(kind).wait_send()
        for copy in give_copies(kind):
            copy.wait_send()

    @pl.when(position < last)
    def _():
        for chunk in range(chunks):
            relay_copy(chunk).wait_send()

    @pl.when(position == last)
    def _():
        for slot in range(micro):
            top_swap(slot).wait_send()


def relay(sections, replicas, ordered, top_grad, up_weight, down_weight, up_moment, down_moment):
    micro, rows, model = ordered.shape[1:]
    width = up_weight.shape[3]
    chunks = 2 * micro
    total = chunks * rows
    layers = replicas // 4
    half_up, half_down = model // (2 * layers), width // (2 * layers)
    held_up, held_down = half_up // 2, half_down // 2
    dma = pltpu.SemaphoreType.DMA
    flops = 2 * 6 * total * model * width
    return pl.pallas_call(
        functools.partial(
            relay_kernel, sections, replicas, micro, rows, model, width, min(512, width), 3
        ),
        out_shape=[
            jax.ShapeDtypeStruct((2, held_up, width), bf16),
            jax.ShapeDtypeStruct((2, held_down, model), bf16),
            jax.ShapeDtypeStruct((held_up, width), f32),
            jax.ShapeDtypeStruct((held_down, model), f32),
        ],
        in_specs=[pl.BlockSpec(memory_space=pl.ANY)] * 6,
        out_specs=[pl.BlockSpec(memory_space=pltpu.VMEM)] * 4,
        scratch_shapes=[
            pltpu.VMEM((model, width), bf16),
            pltpu.VMEM((width, model), bf16),
            pltpu.VMEM((chunks, rows, model), bf16),
            pltpu.VMEM((chunks, rows, width), bf16),
            pltpu.VMEM((chunks, rows, width), bf16),
            pltpu.VMEM((chunks, rows, model), f32),
            pltpu.VMEM((chunks, rows, 128), f32),
            pltpu.VMEM((total, width), bf16),
            pltpu.VMEM((total, model), bf16),
            pltpu.VMEM((chunks, rows, model), bf16),
            pltpu.VMEM((chunks, rows, model), bf16),
            pltpu.VMEM((model, width), bf16),
            pltpu.VMEM((width, model), bf16),
            pltpu.VMEM((2, layers - 1, half_up, width), bf16),
            pltpu.VMEM((2, layers - 1, half_down, model), bf16),
            pltpu.VMEM((half_up, width), bf16),
            pltpu.VMEM((half_down, model), bf16),
            pltpu.VMEM((held_up, width), bf16),
            pltpu.VMEM((held_down, model), bf16),
            pltpu.VMEM((2, held_up, width), bf16),
            pltpu.VMEM((2, held_down, model), bf16),
            pltpu.VMEM((held_up, width), f32),
            pltpu.VMEM((held_down, model), f32),
            pltpu.VMEM((held_up, width), bf16),
            pltpu.VMEM((held_down, model), bf16),
            pltpu.VMEM((held_up, width), bf16),
            pltpu.VMEM((held_down, model), bf16),
            pltpu.VMEM((2, held_up, width), bf16),
            pltpu.VMEM((2, held_down, model), bf16),
            dma((2,)),
            dma((micro,)),
            dma((micro,)),
            dma((micro,)),
            dma((micro,)),
            dma((chunks,)),
            dma((chunks,)),
            dma((2, 3)),
            dma((2,)),
            dma((2,)),
            dma((2, 2, layers - 1)),
            dma((2, 2, layers - 1)),
            dma((2,)),
            dma((2,)),
            dma((2, 3)),
            dma((2, 3)),
        ],
        compiler_params=pltpu.CompilerParams(
            collective_id=0, has_side_effects=True, vmem_limit_bytes=60 * 1024 * 1024
        ),
        cost_estimate=pl.CostEstimate(flops=flops, bytes_accessed=24 << 20, transcendentals=0),
    )(ordered, top_grad, up_weight, down_weight, up_moment, down_moment)


def on_device(section_inputs, top_grad, plan, up_weight, down_weight, up_moment, down_moment):
    ordered = jnp.stack([section_inputs[c, 0][plan[c]] for c in range(2)])
    new_up, new_down, moment_up, moment_down = relay(
        lax.axis_size("section"), lax.axis_size("dp"),
        ordered, top_grad, up_weight, down_weight, up_moment, down_moment,
    )
    return (new_up[:, None], new_down[:, None], moment_up[None], moment_down[None])


def solution(mesh):
    in_specs = (
        P(None, "section", None, "dp", None),
        P(None, None, "dp", None),
        P(),
        P(None, "section", None, None),
        P(None, "section", None, None),
        P("section", "dp", None),
        P("section", "dp", None),
    )
    out_specs = (
        P(None, "section", "dp", None),
        P(None, "section", "dp", None),
        P("section", "dp", None),
        P("section", "dp", None),
    )
    return jax.shard_map(
        on_device, mesh=mesh, in_specs=in_specs, out_specs=out_specs, check_vma=False
    )
```

```python
import functools

import jax
import jax.numpy as jnp
from jax import lax
from jax.experimental import pallas as pl
from jax.experimental.pallas import tpu as pltpu
from jax.sharding import PartitionSpec as P

norm_epsilon = 1e-06
momentum_decay = 0.9
step_size = 0.01
root_half = 0.7071067811865476
inv_root_tau = 0.3989422804014327
MESH = pl.DeviceIdType.MESH
bf16 = jnp.bfloat16
f32 = jnp.float32


def contract_rows(left, right):
    return lax.dot_general(
        left, right, (((0,), (0,)), ((), ())), preferred_element_type=f32
    )


def relay_kernel(
    sections, replicas, micro, rows, model, width, tile, ahead,
    plan_ref, inputs_hbm, top_hbm, up_hbm, down_hbm, moment_up_hbm, moment_down_hbm,
    new_up, new_down, new_moment_up, new_moment_down,
    w_up, w_down, x_buf, x_plan, hidden, slope, normed, scale_buf, grad_pre, grad_low, e_buf, sent,
    part_up, part_down, ring_up, ring_down, pair_up, pair_down, swap_up, swap_down,
    far_up, far_down, moment_up, moment_down, low_up, low_down, their_up, their_down,
    held_up, held_down,
    w_sem, own_sem, swap_send, swap_recv, top_send, e_recv, e_send,
    state_sem, moment_send, moment_recv, ring_send, ring_recv, pair_send, pair_recv,
    give_send, give_recv,
):
    section = lax.axis_index("section")
    replica = lax.axis_index("dp")
    core = lax.rem(replica, 2)
    other = replica + 1 - 2 * core
    side = lax.rem(replica // 2, 2)
    layer = replica // 4
    layers = replicas // 4
    above = lax.rem(replica + 4, replicas)
    below = lax.rem(replica + replicas - 4, replicas)
    beside = replica + 2 - 4 * side
    mirror = sections - 1 - section
    position = jnp.where(core == 0, sections - 1 - section, section)
    step_to = 2 * core - 1
    after = lax.rem(section + step_to + sections, sections)
    before = lax.rem(section - step_to + sections, sections)
    chunks = 2 * micro
    last = sections - 1
    parts = (part_up, part_down)
    rings = (ring_up, ring_down)
    pairs = (pair_up, pair_down)
    swaps = (swap_up, swap_down)
    fars = (far_up, far_down)
    lows = (low_up, low_down)
    theirs = (their_up, their_down)
    moments = (moment_up, moment_down)
    helds = (held_up, held_down)
    halves = (model // (2 * layers), width // (2 * layers))

    w_up_copy = pltpu.make_async_copy(up_hbm.at[core, 0], w_up, w_sem.at[0])
    w_down_copy = pltpu.make_async_copy(down_hbm.at[core, 0], w_down, w_sem.at[1])

    def aligned(start, size):
        return pl.ds(pl.multiple_of(start, size), size)

    def own_copy(slot):
        return pltpu.make_async_copy(
            inputs_hbm.at[core, 0, slot], x_buf.at[2 * slot + core], own_sem.at[slot]
        )

    def remote(src, dst, send, recv, device):
        return pltpu.make_async_remote_copy(
            src_ref=src, dst_ref=dst, send_sem=send, recv_sem=recv,
            device_id=device, device_id_type=MESH,
        )

    def swap_copy(slot):
        return remote(
            inputs_hbm.at[1 - core, 0, slot], x_buf.at[2 * slot + core],
            swap_send.at[slot], swap_recv.at[slot], (section, other),
        )

    def top_own(slot):
        return pltpu.make_async_copy(
            top_hbm.at[core, slot], e_buf.at[2 * slot + core], e_recv.at[2 * slot + core]
        )

    def top_swap(slot):
        return remote(
            top_hbm.at[1 - core, slot], e_buf.at[2 * slot + core],
            top_send.at[slot], e_recv.at[2 * slot + core], (section, other),
        )

    def relay_copy(chunk):
        return remote(
            sent.at[chunk], e_buf.at[chunk], e_send.at[chunk], e_recv.at[chunk], (after, replica)
        )

    def moment_copy(kind):
        return remote(
            lows[kind], theirs[kind], moment_send.at[kind], moment_recv.at[kind], (mirror, replica)
        )

    def ring_block(way, step):
        shift = layers - 1 - step if way == 0 else 1 + step
        return lax.rem(layer + shift, layers)

    def ring_copy(kind, way, step):
        half = halves[kind]
        start = ring_block(way, step) * 2 * half + way * half
        return remote(
            parts[kind].at[aligned(start, half), :], rings[kind].at[way, step],
            ring_send.at[kind, way, step], ring_recv.at[kind, way, step],
            (section, above if way == 0 else below),
        )

    def pair_copy(kind):
        half = halves[kind]
        start = layer * 2 * half + (1 - side) * half
        return remote(
            parts[kind].at[aligned(start, half), :], pairs[kind],
            pair_send.at[kind], pair_recv.at[kind], (section, beside),
        )

    def final_rows(kind, which):
        half = halves[kind]
        quarter = half // 2
        return aligned(layer * 2 * half + side * half + which * quarter, quarter)

    def give_copies(kind):
        return (
            remote(
                parts[kind].at[final_rows(kind, core), :], fars[kind].at[0],
                give_send.at[kind, 0], give_recv.at[kind, 0], (mirror, replica),
            ),
            remote(
                parts[kind].at[final_rows(kind, 1 - core), :], fars[kind].at[1],
                give_send.at[kind, 1], give_recv.at[kind, 1], (mirror, other),
            ),
            remote(
                parts[kind].at[final_rows(kind, 1 - core), :], swaps[kind],
                give_send.at[kind, 2], give_recv.at[kind, 2], (section, other),
            ),
        )

    state_copies = []
    for kind, (held_hbm, moment_hbm) in enumerate(
        ((up_hbm, moment_up_hbm), (down_hbm, moment_down_hbm))
    ):
        state_copies.append(
            pltpu.make_async_copy(moment_hbm.at[0], moments[kind], state_sem.at[kind, 0])
        )
        count = helds[kind].shape[1]
        for c in range(2):
            state_copies.append(
                pltpu.make_async_copy(
                    held_hbm.at[c, 0, aligned(replica * count, count), :],
                    helds[kind].at[c], state_sem.at[kind, 1 + c],
                )
            )

    w_up_copy.start()
    for slot in range(micro):
        own_copy(slot).start()
    w_down_copy.start()
    for copy in state_copies:
        copy.start()

    barrier = pltpu.get_barrier_semaphore()
    for device in (
        (after, replica), (before, replica), (section, other), (section, above),
        (section, below), (section, beside), (mirror, replica), (mirror, other),
    ):
        pl.semaphore_signal(barrier, inc=1, device_id=device, device_id_type=MESH)
    pl.semaphore_wait(barrier, 8)

    @pl.when(position == last)
    def _():
        for slot in range(micro):
            top_swap(slot).start()

    for slot in range(micro):
        swap_copy(slot).start()

    @pl.when(position == 0)
    def _():
        for slot in range(micro):
            top_own(slot).start()

    turned_down, turned_up = part_up, part_down
    across = min(256, model)

    w_up_copy.wait()

    @pl.loop(0, width // across)
    def _(t):
        cols = aligned(t * across, across)
        turned_up[cols, :] = w_up[:, cols].T

    w_down_copy.wait()

    @pl.loop(0, width // across)
    def _(t):
        cols = aligned(t * across, across)
        turned_down[:, cols] = w_down[cols, :].T

    for slot in range(micro):
        own_copy(slot).wait()
        swap_copy(slot).wait()

    def forward(chunk):
        x = x_buf[2 * plan_ref[core, chunk // 2] + lax.rem(chunk, 2)]
        x_plan[chunk] = x

        for n in range(width // tile):
            cols = pl.ds(n * tile, tile)
            preact = jnp.dot(x, w_up[:, cols], preferred_element_type=f32)
            cdf = 0.5 * (1.0 + lax.erf(preact * root_half))
            hidden[chunk, :, cols] = (preact * cdf).astype(bf16)
            grown = cdf + preact * jnp.exp(-0.5 * preact * preact) * inv_root_tau
            slope[chunk, :, cols] = grown.astype(bf16)
        summed = x.astype(f32) + jnp.dot(hidden[chunk], w_down[...], preferred_element_type=f32)
        centre = summed - jnp.mean(summed, axis=-1, keepdims=True)
        scale_inv = lax.rsqrt(jnp.mean(centre * centre, axis=-1, keepdims=True) + norm_epsilon)
        normed[chunk] = centre * scale_inv
        scale_buf[chunk] = jnp.broadcast_to(scale_inv, (rows, 128))

    def backward(chunk):
        pltpu.make_async_copy(sent.at[chunk], e_buf.at[chunk], e_recv.at[chunk]).wait()
        upstream = e_buf[chunk].astype(f32)
        y = normed[chunk]
        scale_inv = scale_buf[chunk][:, :1]
        grad_sum = scale_inv * (
            upstream
            - jnp.mean(upstream, axis=-1, keepdims=True)
            - y * jnp.mean(upstream * y, axis=-1, keepdims=True)
        )
        low = grad_sum.astype(bf16)
        place = aligned(chunk * rows, rows)
        grad_low[place, :] = low
        for n in range(width // tile):
            cols = pl.ds(n * tile, tile)
            grad = jnp.dot(low, turned_down[:, cols], preferred_element_type=f32)
            grad = grad * slope[chunk, :, cols].astype(f32)
            grad_pre[place, cols] = grad.astype(bf16)

        @pl.when(position < last)
        def _():
            grad_in = jnp.dot(grad_pre[place, :], turned_up[...], preferred_element_type=f32)
            sent[chunk] = (grad_sum + grad_in).astype(bf16)
            relay_copy(chunk).start()

    lead = jnp.minimum(chunks, ahead * position)

    @pl.loop(0, 2 * chunks)
    def _(step):
        @pl.when(step < chunks)
        def _():
            forward(step)

        back = step - lead

        @pl.when(jnp.logical_and(back >= 0, back < chunks))
        def _():
            backward(back)

        @pl.when(step == chunks - 1)
        def _():
            for copy in state_copies:
                copy.wait()
            for kind in range(2):
                lows[kind][...] = moments[kind][...].astype(bf16)
                moment_copy(kind).start()

    total = chunks * rows
    span = min(256, 2 * halves[0])

    def up_block(block):
        @pl.loop(0, 2 * halves[0] // span)
        def _(t):
            cols = aligned(block * 2 * halves[0] + t * span, span)
            left = x_plan[:, :, cols].reshape(total, span)
            part_up[cols, :] = contract_rows(left, grad_pre[...]).astype(bf16)

    def down_block(block):
        @pl.loop(0, 2 * halves[1] // span)
        def _(t):
            cols = aligned(block * 2 * halves[1] + t * span, span)
            left = hidden[:, :, cols].reshape(total, span)
            part_down[cols, :] = contract_rows(left, grad_low[...]).astype(bf16)

    def blocks(fill, shifts):
        @pl.loop(0, len(shifts))
        def _(i):
            shift = jnp.where(i == 0, shifts[0], shifts[-1])
            fill(lax.rem(layer + shift, layers))

    def first(kind, fill):
        fill(ring_block(0, 0))
        ring_copy(kind, 0, 0).start()
        fill(ring_block(1, 0))
        ring_copy(kind, 1, 0).start()

    def add_rows(kind, start, size, value):
        place = aligned(start, size)
        held = parts[kind][place, :].astype(f32) + value.astype(f32)
        parts[kind][place, :] = held.astype(bf16)

    def turn(kind, step):
        for way in range(2):
            ring_copy(kind, way, step).wait_recv()
            half = halves[kind]
            start = ring_block(way, step + 1) * 2 * half + way * half
            add_rows(kind, start, half, rings[kind][way, step])
            if step < layers - 2:
                ring_copy(kind, way, step + 1).start()

    def settle(kind):
        half = halves[kind]
        pair_copy(kind).start()
        pair_copy(kind).wait_recv()
        add_rows(kind, layer * 2 * half + side * half, half, pairs[kind][...])
        for copy in give_copies(kind):
            copy.start()

    rest = [2, 0]
    first(0, up_block)
    blocks(up_block, rest)
    first(1, down_block)
    turn(0, 0)
    blocks(down_block, rest)
    turn(1, 0)
    for step in range(1, layers - 2):
        turn(0, step)
        turn(1, step)
    turn(0, layers - 2)
    settle(0)
    turn(1, layers - 2)
    settle(1)

    for kind in range(2):
        moment_copy(kind).wait()

    for kind, (out, out_moment) in enumerate(
        ((new_up, new_moment_up), (new_down, new_moment_down))
    ):
        for copy in give_copies(kind):
            copy.wait_recv()
        own = parts[kind][final_rows(kind, core), :].astype(f32)
        got = swaps[kind][...].astype(f32)
        same = fars[kind][0].astype(f32)
        cross = fars[kind][1].astype(f32)
        zero = core == 0
        grad = jnp.where(zero, own + cross, got + same)
        grad_mirror = jnp.where(zero, got + same, own + cross)
        moment = momentum_decay * moments[kind][...] + grad
        out_moment[...] = moment
        out[0] = (helds[kind][0].astype(f32) - step_size * moment).astype(bf16)
        mirrored = momentum_decay * theirs[kind][...].astype(f32) + grad_mirror
        out[1] = (helds[kind][1].astype(f32) - step_size * mirrored).astype(bf16)

    for kind in range(2):
        for way in range(2):
            for step in range(layers - 1):
                ring_copy(kind, way, step).wait_send()
        pair_copy(kind).wait_send()
        for copy in give_copies(kind):
            copy.wait_send()

    @pl.when(position < last)
    def _():
        for chunk in range(chunks):
            relay_copy(chunk).wait_send()

    @pl.when(position == last)
    def _():
        for slot in range(micro):
            top_swap(slot).wait_send()


def relay(sections, replicas, plan, inputs, top_grad, up_weight, down_weight, up_moment, down_moment):
    micro, rows, model = inputs.shape[2:]
    width = up_weight.shape[3]
    chunks = 2 * micro
    total = chunks * rows
    layers = replicas // 4
    half_up, half_down = model // (2 * layers), width // (2 * layers)
    held_up, held_down = half_up // 2, half_down // 2
    dma = pltpu.SemaphoreType.DMA
    flops = 2 * 6 * total * model * width
    return pl.pallas_call(
        functools.partial(
            relay_kernel, sections, replicas, micro, rows, model, width, min(512, width), 3
        ),
        out_shape=[
            jax.ShapeDtypeStruct((2, held_up, width), bf16),
            jax.ShapeDtypeStruct((2, held_down, model), bf16),
            jax.ShapeDtypeStruct((held_up, width), f32),
            jax.ShapeDtypeStruct((held_down, model), f32),
        ],
        in_specs=[pl.BlockSpec(memory_space=pltpu.SMEM)] + [pl.BlockSpec(memory_space=pl.ANY)] * 6,
        out_specs=[pl.BlockSpec(memory_space=pltpu.VMEM)] * 4,
        scratch_shapes=[
            pltpu.VMEM((model, width), bf16),
            pltpu.VMEM((width, model), bf16),
            pltpu.VMEM((chunks, rows, model), bf16),
            pltpu.VMEM((chunks, rows, model), bf16),
            pltpu.VMEM((chunks, rows, width), bf16),
            pltpu.VMEM((chunks, rows, width), bf16),
            pltpu.VMEM((chunks, rows, model), f32),
            pltpu.VMEM((chunks, rows, 128), f32),
            pltpu.VMEM((total, width), bf16),
            pltpu.VMEM((total, model), bf16),
            pltpu.VMEM((chunks, rows, model), bf16),
            pltpu.VMEM((chunks, rows, model), bf16),
            pltpu.VMEM((model, width), bf16),
            pltpu.VMEM((width, model), bf16),
            pltpu.VMEM((2, layers - 1, half_up, width), bf16),
            pltpu.VMEM((2, layers - 1, half_down, model), bf16),
            pltpu.VMEM((half_up, width), bf16),
            pltpu.VMEM((half_down, model), bf16),
            pltpu.VMEM((held_up, width), bf16),
            pltpu.VMEM((held_down, model), bf16),
            pltpu.VMEM((2, held_up, width), bf16),
            pltpu.VMEM((2, held_down, model), bf16),
            pltpu.VMEM((held_up, width), f32),
            pltpu.VMEM((held_down, model), f32),
            pltpu.VMEM((held_up, width), bf16),
            pltpu.VMEM((held_down, model), bf16),
            pltpu.VMEM((held_up, width), bf16),
            pltpu.VMEM((held_down, model), bf16),
            pltpu.VMEM((2, held_up, width), bf16),
            pltpu.VMEM((2, held_down, model), bf16),
            dma((2,)),
            dma((micro,)),
            dma((micro,)),
            dma((micro,)),
            dma((micro,)),
            dma((chunks,)),
            dma((chunks,)),
            dma((2, 3)),
            dma((2,)),
            dma((2,)),
            dma((2, 2, layers - 1)),
            dma((2, 2, layers - 1)),
            dma((2,)),
            dma((2,)),
            dma((2, 3)),
            dma((2, 3)),
        ],
        compiler_params=pltpu.CompilerParams(
            collective_id=0, has_side_effects=True, vmem_limit_bytes=60 * 1024 * 1024
        ),
        cost_estimate=pl.CostEstimate(flops=flops, bytes_accessed=24 << 20, transcendentals=0),
    )(plan, inputs, top_grad, up_weight, down_weight, up_moment, down_moment)


def hand_on_kernel(*refs):
    count = len(refs) // 2
    for source, target in zip(refs[:count], refs[count:]):
        target[...] = source[...]


def hand_on(*values):
    return pl.pallas_call(
        hand_on_kernel,
        out_shape=[jax.ShapeDtypeStruct(v.shape, v.dtype) for v in values],
        in_specs=[pl.BlockSpec(memory_space=pltpu.VMEM)] * len(values),
        out_specs=[pl.BlockSpec(memory_space=pltpu.VMEM)] * len(values),
        compiler_params=pltpu.CompilerParams(vmem_limit_bytes=8 << 20),
    )(*values)


def on_device(section_inputs, top_grad, plan, up_weight, down_weight, up_moment, down_moment):
    new_up, new_down, moment_up, moment_down = hand_on(*relay(
        lax.axis_size("section"), lax.axis_size("dp"), plan, section_inputs,
        top_grad, up_weight, down_weight, up_moment, down_moment,
    ))
    return (new_up[:, None], new_down[:, None], moment_up[None], moment_down[None])


def solution(mesh):
    in_specs = (
        P(None, "section", None, "dp", None),
        P(None, None, "dp", None),
        P(),
        P(None, "section", None, None),
        P(None, "section", None, None),
        P("section", "dp", None),
        P("section", "dp", None),
    )
    out_specs = (
        P(None, "section", "dp", None),
        P(None, "section", "dp", None),
        P("section", "dp", None),
        P("section", "dp", None),
    )
    return jax.shard_map(
        on_device, mesh=mesh, in_specs=in_specs, out_specs=out_specs, check_vma=False
    )
```

```python
import functools

import jax
import jax.numpy as jnp
from jax import lax
from jax.experimental import pallas as pl
from jax.experimental.pallas import tpu as pltpu
from jax.sharding import PartitionSpec as P

norm_epsilon = 1e-06
momentum_decay = 0.9
step_size = 0.01
root_half = 0.7071067811865476
inv_root_tau = 0.3989422804014327
MESH = pl.DeviceIdType.MESH
bf16 = jnp.bfloat16
f32 = jnp.float32


def contract_rows(left, right):
    return lax.dot_general(
        left, right, (((0,), (0,)), ((), ())), preferred_element_type=f32
    )


def relay_kernel(
    sections, replicas, micro, rows, model, width, tile, ahead,
    plan_ref, inputs_hbm, top_hbm, up_hbm, down_hbm, moment_up_hbm, moment_down_hbm,
    new_up, new_down, new_moment_up, new_moment_down,
    w_up, w_down, x_buf, x_plan, hidden, slope, normed, scale_buf, grad_pre, grad_low, e_buf, sent,
    part_up, part_down, ring_up, ring_c, ring_d, pair_up, pair_c, pair_d, swap_up, swap_down,
    far_up, far_down, moment_up, moment_down, low_up, low_down, their_up, their_down,
    held_up, held_down,
    w_sem, own_sem, swap_send, swap_recv, top_send, e_recv, e_send,
    state_sem, moment_send, moment_recv, ring_send, ring_recv, pair_send, pair_recv,
    give_send, give_recv,
):
    section = lax.axis_index("section")
    replica = lax.axis_index("dp")
    core = lax.rem(replica, 2)
    other = replica + 1 - 2 * core
    side = lax.rem(replica // 2, 2)
    layer = replica // 4
    layers = replicas // 4
    above = lax.rem(replica + 4, replicas)
    below = lax.rem(replica + replicas - 4, replicas)
    beside = replica + 2 - 4 * side
    mirror = sections - 1 - section
    position = jnp.where(core == 0, sections - 1 - section, section)
    step_to = 2 * core - 1
    after = lax.rem(section + step_to + sections, sections)
    before = lax.rem(section - step_to + sections, sections)
    chunks = 2 * micro
    last = sections - 1
    parts = (part_up, part_down)
    rings = (ring_up.at[0], ring_up.at[1], ring_c, ring_d)
    pairs = (pair_up.at[0], pair_up.at[1], pair_c)
    kinds = (0, 0, 1, 1)
    spans = tuple(
        pl.ds((piece % 2) * (size // 2), size // 2)
        for piece, size in enumerate((width, width, model, model))
    )
    swaps = (swap_up, swap_down)
    fars = (far_up, far_down)
    lows = (low_up, low_down)
    theirs = (their_up, their_down)
    moments = (moment_up, moment_down)
    helds = (held_up, held_down)
    halves = (model // (2 * layers), width // (2 * layers))

    w_up_copy = pltpu.make_async_copy(up_hbm.at[core, 0], w_up, w_sem.at[0])
    w_down_copy = pltpu.make_async_copy(down_hbm.at[core, 0], w_down, w_sem.at[1])

    def aligned(start, size):
        return pl.ds(pl.multiple_of(start, size), size)

    def own_copy(slot):
        return pltpu.make_async_copy(
            inputs_hbm.at[core, 0, slot], x_buf.at[2 * slot + core], own_sem.at[slot]
        )

    def remote(src, dst, send, recv, device):
        return pltpu.make_async_remote_copy(
            src_ref=src, dst_ref=dst, send_sem=send, recv_sem=recv,
            device_id=device, device_id_type=MESH,
        )

    def swap_copy(slot):
        return remote(
            inputs_hbm.at[1 - core, 0, slot], x_buf.at[2 * slot + core],
            swap_send.at[slot], swap_recv.at[slot], (section, other),
        )

    def top_own(slot):
        return pltpu.make_async_copy(
            top_hbm.at[core, slot], e_buf.at[2 * slot + core], e_recv.at[2 * slot + core]
        )

    def top_swap(slot):
        return remote(
            top_hbm.at[1 - core, slot], e_buf.at[2 * slot + core],
            top_send.at[slot], e_recv.at[2 * slot + core], (section, other),
        )

    def relay_copy(chunk):
        return remote(
            sent.at[chunk], e_buf.at[chunk], e_send.at[chunk], e_recv.at[chunk], (after, replica)
        )

    def moment_copy(kind):
        return remote(
            lows[kind], theirs[kind], moment_send.at[kind], moment_recv.at[kind], (mirror, replica)
        )

    def ring_block(way, step):
        shift = layers - 1 - step if way == 0 else 1 + step
        return lax.rem(layer + shift, layers)

    def ring_rows(piece, way, step):
        half = halves[kinds[piece]]
        start = ring_block(way, step) * 2 * half
        if piece == 3:
            return aligned(start + side * half + way * (half // 2), half // 2)
        return aligned(start + way * half, half)

    def ring_copy(piece, way, step):
        return remote(
            parts[kinds[piece]].at[ring_rows(piece, way, step), spans[piece]],
            rings[piece].at[way, step],
            ring_send.at[piece, way, step], ring_recv.at[piece, way, step],
            (section, above if way == 0 else below),
        )

    def pair_copy(piece):
        half = halves[kinds[piece]]
        start = layer * 2 * half + (1 - side) * half
        return remote(
            parts[kinds[piece]].at[aligned(start, half), spans[piece]], pairs[piece],
            pair_send.at[piece], pair_recv.at[piece], (section, beside),
        )

    def early_copy(block):
        half = halves[1]
        start = block * 2 * half + (1 - side) * half
        return remote(
            part_down.at[aligned(start, half), spans[3]], pair_d.at[block],
            pair_send.at[3 + block], pair_recv.at[3 + block], (section, beside),
        )

    def final_rows(kind, which):
        half = halves[kind]
        quarter = half // 2
        return aligned(layer * 2 * half + side * half + which * quarter, quarter)

    def give_copies(piece):
        kind = kinds[piece]
        cols = spans[piece]
        return (
            remote(
                parts[kind].at[final_rows(kind, core), cols], fars[kind].at[0, :, cols],
                give_send.at[piece, 0], give_recv.at[piece, 0], (mirror, replica),
            ),
            remote(
                parts[kind].at[final_rows(kind, 1 - core), cols], fars[kind].at[1, :, cols],
                give_send.at[piece, 1], give_recv.at[piece, 1], (mirror, other),
            ),
            remote(
                parts[kind].at[final_rows(kind, 1 - core), cols], swaps[kind].at[:, cols],
                give_send.at[piece, 2], give_recv.at[piece, 2], (section, other),
            ),
        )

    state_copies = []
    for kind, (held_hbm, moment_hbm) in enumerate(
        ((up_hbm, moment_up_hbm), (down_hbm, moment_down_hbm))
    ):
        state_copies.append(
            pltpu.make_async_copy(moment_hbm.at[0], moments[kind], state_sem.at[kind, 0])
        )
        count = helds[kind].shape[1]
        for c in range(2):
            state_copies.append(
                pltpu.make_async_copy(
                    held_hbm.at[c, 0, aligned(replica * count, count), :],
                    helds[kind].at[c], state_sem.at[kind, 1 + c],
                )
            )

    w_up_copy.start()
    for slot in range(micro):
        own_copy(slot).start()
    w_down_copy.start()
    for copy in state_copies:
        copy.start()

    barrier = pltpu.get_barrier_semaphore()
    for device in (
        (after, replica), (before, replica), (section, other), (section, above),
        (section, below), (section, beside), (mirror, replica), (mirror, other),
    ):
        pl.semaphore_signal(barrier, inc=1, device_id=device, device_id_type=MESH)
    pl.semaphore_wait(barrier, 8)

    @pl.when(position == last)
    def _():
        for slot in range(micro):
            top_swap(slot).start()

    for slot in range(micro):
        swap_copy(slot).start()

    @pl.when(position == 0)
    def _():
        for slot in range(micro):
            top_own(slot).start()

    turned_down, turned_up = part_up, part_down
    across = min(256, model)

    w_up_copy.wait()

    @pl.loop(0, width // across)
    def _(t):
        cols = aligned(t * across, across)
        turned_up[cols, :] = w_up[:, cols].T

    w_down_copy.wait()

    @pl.loop(0, width // across)
    def _(t):
        cols = aligned(t * across, across)
        turned_down[:, cols] = w_down[cols, :].T

    for slot in range(micro):
        own_copy(slot).wait()
        swap_copy(slot).wait()

    def forward(chunk):
        x = x_buf[2 * plan_ref[core, chunk // 2] + lax.rem(chunk, 2)]
        x_plan[chunk] = x

        for n in range(width // tile):
            cols = pl.ds(n * tile, tile)
            preact = jnp.dot(x, w_up[:, cols], preferred_element_type=f32)
            cdf = 0.5 * (1.0 + lax.erf(preact * root_half))
            hidden[chunk, :, cols] = (preact * cdf).astype(bf16)
            grown = cdf + preact * jnp.exp(-0.5 * preact * preact) * inv_root_tau
            slope[chunk, :, cols] = grown.astype(bf16)
        summed = x.astype(f32) + jnp.dot(hidden[chunk], w_down[...], preferred_element_type=f32)
        centre = summed - jnp.mean(summed, axis=-1, keepdims=True)
        scale_inv = lax.rsqrt(jnp.mean(centre * centre, axis=-1, keepdims=True) + norm_epsilon)
        normed[chunk] = centre * scale_inv
        scale_buf[chunk] = jnp.broadcast_to(scale_inv, (rows, 128))

    def backward(chunk):
        pltpu.make_async_copy(sent.at[chunk], e_buf.at[chunk], e_recv.at[chunk]).wait()
        upstream = e_buf[chunk].astype(f32)
        y = normed[chunk]
        scale_inv = scale_buf[chunk][:, :1]
        grad_sum = scale_inv * (
            upstream
            - jnp.mean(upstream, axis=-1, keepdims=True)
            - y * jnp.mean(upstream * y, axis=-1, keepdims=True)
        )
        low = grad_sum.astype(bf16)
        place = aligned(chunk * rows, rows)
        grad_low[place, :] = low
        for n in range(width // tile):
            cols = pl.ds(n * tile, tile)
            grad = jnp.dot(low, turned_down[:, cols], preferred_element_type=f32)
            grad = grad * slope[chunk, :, cols].astype(f32)
            grad_pre[place, cols] = grad.astype(bf16)

        @pl.when(position < last)
        def _():
            grad_in = jnp.dot(grad_pre[place, :], turned_up[...], preferred_element_type=f32)
            sent[chunk] = (grad_sum + grad_in).astype(bf16)
            relay_copy(chunk).start()

    lead = jnp.minimum(chunks, ahead * position)

    @pl.loop(0, 2 * chunks)
    def _(step):
        @pl.when(step < chunks)
        def _():
            forward(step)

        back = step - lead

        @pl.when(jnp.logical_and(back >= 0, back < chunks))
        def _():
            backward(back)

        @pl.when(step == chunks - 1)
        def _():
            for copy in state_copies:
                copy.wait()
            for kind in range(2):
                lows[kind][...] = moments[kind][...].astype(bf16)
                moment_copy(kind).start()

    total = chunks * rows
    up_rows, down_rows = 2 * halves[0], halves[1]

    def up_block(block):
        cols = aligned(block * up_rows, up_rows)
        left = x_plan[:, :, cols].reshape(total, up_rows)
        part_up[cols, :] = contract_rows(left, grad_pre[...]).astype(bf16)

    def down_block(block, which):
        cols = aligned(block * 2 * down_rows + which * down_rows, down_rows)
        left = hidden[:, :, cols].reshape(total, down_rows)
        part_down[cols, :] = contract_rows(left, grad_low[...]).astype(bf16)

    def add_rows(piece, place, value):
        part = parts[kinds[piece]]
        cols = spans[piece]
        part[place, cols] = (part[place, cols].astype(f32) + value.astype(f32)).astype(bf16)

    def turn(piece, step):
        for way in range(2):
            ring_copy(piece, way, step).wait_recv()
            add_rows(piece, ring_rows(piece, way, step + 1), rings[piece][way, step])
            if step < layers - 2:
                ring_copy(piece, way, step + 1).start()

    def give(piece):
        for copy in give_copies(piece):
            copy.start()

    def settle(piece):
        half = halves[kinds[piece]]
        pair_copy(piece).wait_recv()
        add_rows(piece, aligned(layer * 2 * half + side * half, half), pairs[piece][...])
        give(piece)

    def update(kind, out, out_moment):
        for piece in (2 * kind, 2 * kind + 1):
            for copy in give_copies(piece):
                copy.wait_recv()
        own = parts[kind][final_rows(kind, core), :].astype(f32)
        got = swaps[kind][...].astype(f32)
        same = fars[kind][0].astype(f32)
        cross = fars[kind][1].astype(f32)
        zero = core == 0
        grad = jnp.where(zero, own + cross, got + same)
        grad_mirror = jnp.where(zero, got + same, own + cross)
        moment = momentum_decay * moments[kind][...] + grad
        out_moment[...] = moment
        out[0] = (helds[kind][0].astype(f32) - step_size * moment).astype(bf16)
        mirrored = momentum_decay * theirs[kind][...].astype(f32) + grad_mirror
        out[1] = (helds[kind][1].astype(f32) - step_size * mirrored).astype(bf16)

    order = (layers - 1, 1, 2, 0)

    @pl.loop(0, 2)
    def _(i):
        up_block(lax.rem(layer + jnp.where(i == 0, order[0], order[1]), layers))

        @pl.when(i == 0)
        def _():
            ring_copy(0, 0, 0).start()
            ring_copy(1, 0, 0).start()

        @pl.when(i == 1)
        def _():
            ring_copy(0, 1, 0).start()
            ring_copy(1, 1, 0).start()

    @pl.loop(0, layers)
    def _(i):
        shift = jnp.where(i == 0, order[0], jnp.where(i == 1, order[1], 2 * (3 - i)))
        block = lax.rem(layer + shift, layers)
        down_block(block, 1 - side)
        early_copy(block).start()

    @pl.loop(0, 2)
    def _(i):
        up_block(lax.rem(layer + jnp.where(i == 0, order[2], order[3]), layers))

    @pl.loop(0, 2)
    def _(i):
        down_block(lax.rem(layer + i, layers), side)

    turn(0, 0)
    turn(1, 0)

    @pl.loop(2, layers)
    def _(i):
        down_block(lax.rem(layer + i, layers), side)

    turn(0, 1)
    turn(1, 1)
    for way in range(2):
        ring_copy(2, way, 0).start()
    turn(0, 2)
    pair_copy(0).start()
    turn(1, 2)
    pair_copy(1).start()

    @pl.loop(0, layers)
    def _(block):
        early_copy(block).wait_recv()
        add_rows(3, aligned(block * 2 * down_rows + side * down_rows, down_rows), pair_d[block])

    for way in range(2):
        ring_copy(3, way, 0).start()
    settle(0)
    turn(2, 0)
    settle(1)
    turn(3, 0)
    turn(2, 1)
    turn(3, 1)
    turn(2, 2)
    pair_copy(2).start()
    turn(3, 2)
    give(3)
    settle(2)
    for kind in range(2):
        moment_copy(kind).wait()
    update(0, new_up, new_moment_up)
    update(1, new_down, new_moment_down)

    for piece in range(4):
        for way in range(2):
            for step in range(layers - 1):
                ring_copy(piece, way, step).wait_send()
        for copy in give_copies(piece):
            copy.wait_send()
    for piece in range(3):
        pair_copy(piece).wait_send()
    for block in range(layers):
        early_copy(block).wait_send()

    @pl.when(position < last)
    def _():
        for chunk in range(chunks):
            relay_copy(chunk).wait_send()

    @pl.when(position == last)
    def _():
        for slot in range(micro):
            top_swap(slot).wait_send()


def relay(sections, replicas, plan, inputs, top_grad, up_weight, down_weight, up_moment, down_moment):
    micro, rows, model = inputs.shape[2:]
    width = up_weight.shape[3]
    chunks = 2 * micro
    total = chunks * rows
    layers = replicas // 4
    half_up, half_down = model // (2 * layers), width // (2 * layers)
    held_up, held_down = half_up // 2, half_down // 2
    dma = pltpu.SemaphoreType.DMA
    flops = 2 * 6 * total * model * width
    return pl.pallas_call(
        functools.partial(
            relay_kernel, sections, replicas, micro, rows, model, width, min(512, width), 3
        ),
        out_shape=[
            jax.ShapeDtypeStruct((2, held_up, width), bf16),
            jax.ShapeDtypeStruct((2, held_down, model), bf16),
            jax.ShapeDtypeStruct((held_up, width), f32),
            jax.ShapeDtypeStruct((held_down, model), f32),
        ],
        in_specs=[pl.BlockSpec(memory_space=pltpu.SMEM)] + [pl.BlockSpec(memory_space=pl.ANY)] * 6,
        out_specs=[pl.BlockSpec(memory_space=pltpu.VMEM)] * 4,
        scratch_shapes=[
            pltpu.VMEM((model, width), bf16),
            pltpu.VMEM((width, model), bf16),
            pltpu.VMEM((chunks, rows, model), bf16),
            pltpu.VMEM((chunks, rows, model), bf16),
            pltpu.VMEM((chunks, rows, width), bf16),
            pltpu.VMEM((chunks, rows, width), bf16),
            pltpu.VMEM((chunks, rows, model), f32),
            pltpu.VMEM((chunks, rows, 128), f32),
            pltpu.VMEM((total, width), bf16),
            pltpu.VMEM((total, model), bf16),
            pltpu.VMEM((chunks, rows, model), bf16),
            pltpu.VMEM((chunks, rows, model), bf16),
            pltpu.VMEM((model, width), bf16),
            pltpu.VMEM((width, model), bf16),
            pltpu.VMEM((2, 2, layers - 1, half_up, width // 2), bf16),
            pltpu.VMEM((2, layers - 1, half_down, model // 2), bf16),
            pltpu.VMEM((2, layers - 1, half_down // 2, model // 2), bf16),
            pltpu.VMEM((2, half_up, width // 2), bf16),
            pltpu.VMEM((half_down, model // 2), bf16),
            pltpu.VMEM((layers, half_down, model // 2), bf16),
            pltpu.VMEM((held_up, width), bf16),
            pltpu.VMEM((held_down, model), bf16),
            pltpu.VMEM((2, held_up, width), bf16),
            pltpu.VMEM((2, held_down, model), bf16),
            pltpu.VMEM((held_up, width), f32),
            pltpu.VMEM((held_down, model), f32),
            pltpu.VMEM((held_up, width), bf16),
            pltpu.VMEM((held_down, model), bf16),
            pltpu.VMEM((held_up, width), bf16),
            pltpu.VMEM((held_down, model), bf16),
            pltpu.VMEM((2, held_up, width), bf16),
            pltpu.VMEM((2, held_down, model), bf16),
            dma((2,)),
            dma((micro,)),
            dma((micro,)),
            dma((micro,)),
            dma((micro,)),
            dma((chunks,)),
            dma((chunks,)),
            dma((2, 3)),
            dma((2,)),
            dma((2,)),
            dma((4, 2, layers - 1)),
            dma((4, 2, layers - 1)),
            dma((3 + layers,)),
            dma((3 + layers,)),
            dma((4, 3)),
            dma((4, 3)),
        ],
        compiler_params=pltpu.CompilerParams(
            collective_id=0, has_side_effects=True, vmem_limit_bytes=60 * 1024 * 1024
        ),
        cost_estimate=pl.CostEstimate(flops=flops, bytes_accessed=24 << 20, transcendentals=0),
    )(plan, inputs, top_grad, up_weight, down_weight, up_moment, down_moment)


def hand_on_kernel(*refs):
    count = len(refs) // 2
    for source, target in zip(refs[:count], refs[count:]):
        target[...] = source[...]


def hand_on(*values):
    return pl.pallas_call(
        hand_on_kernel,
        out_shape=[jax.ShapeDtypeStruct(v.shape, v.dtype) for v in values],
        in_specs=[pl.BlockSpec(memory_space=pltpu.VMEM)] * len(values),
        out_specs=[pl.BlockSpec(memory_space=pltpu.VMEM)] * len(values),
        compiler_params=pltpu.CompilerParams(vmem_limit_bytes=8 << 20),
    )(*values)


def on_device(section_inputs, top_grad, plan, up_weight, down_weight, up_moment, down_moment):
    new_up, new_down, moment_up, moment_down = hand_on(*relay(
        lax.axis_size("section"), lax.axis_size("dp"), plan, section_inputs,
        top_grad, up_weight, down_weight, up_moment, down_moment,
    ))
    return (new_up[:, None], new_down[:, None], moment_up[None], moment_down[None])


def solution(mesh):
    in_specs = (
        P(None, "section", None, "dp", None),
        P(None, None, "dp", None),
        P(),
        P(None, "section", None, None),
        P(None, "section", None, None),
        P("section", "dp", None),
        P("section", "dp", None),
    )
    out_specs = (
        P(None, "section", "dp", None),
        P(None, "section", "dp", None),
        P("section", "dp", None),
        P("section", "dp", None),
    )
    return jax.shard_map(
        on_device, mesh=mesh, in_specs=in_specs, out_specs=out_specs, check_vma=False
    )
```

```python
import functools

import jax
import jax.numpy as jnp
from jax import lax
from jax.experimental import pallas as pl
from jax.experimental.pallas import tpu as pltpu
from jax.sharding import PartitionSpec as P

norm_epsilon = 1e-06
momentum_decay = 0.9
step_size = 0.01
root_half = 0.7071067811865476
inv_root_tau = 0.3989422804014327
MESH = pl.DeviceIdType.MESH
bf16 = jnp.bfloat16
f32 = jnp.float32


def contract_rows(left, right):
    return lax.dot_general(
        left, right, (((0,), (0,)), ((), ())), preferred_element_type=f32
    )


def relay_kernel(
    sections, replicas, micro, rows, model, width, tile, ahead,
    plan_ref, inputs_hbm, top_hbm, up_hbm, down_hbm, moment_up_hbm, moment_down_hbm,
    new_up, new_down, new_moment_up, new_moment_down,
    w_up, w_down, x_buf, x_plan, hidden, slope, normed, scale_buf, grad_pre, grad_low, e_buf, sent,
    part_up, part_down, ring_up, ring_c, ring_d, pair_up, pair_c, pair_d, swap_up, swap_down,
    far_up, far_down, moment_up, moment_down, low_up, low_down, their_up, their_down,
    held_up, held_down,
    w_sem, own_sem, swap_send, swap_recv, top_send, e_recv, e_send,
    state_sem, moment_send, moment_recv, ring_send, ring_recv, pair_send, pair_recv,
    give_send, give_recv,
):
    section = lax.axis_index("section")
    replica = lax.axis_index("dp")
    core = lax.rem(replica, 2)
    other = replica + 1 - 2 * core
    side = lax.rem(replica // 2, 2)
    layer = replica // 4
    layers = replicas // 4
    above = lax.rem(replica + 4, replicas)
    below = lax.rem(replica + replicas - 4, replicas)
    beside = replica + 2 - 4 * side
    mirror = sections - 1 - section
    position = jnp.where(core == 0, sections - 1 - section, section)
    step_to = 2 * core - 1
    after = lax.rem(section + step_to + sections, sections)
    before = lax.rem(section - step_to + sections, sections)
    chunks = 2 * micro
    last = sections - 1
    parts = (part_up, part_down)
    rings = (ring_up.at[0], ring_up.at[1], ring_c, ring_d)
    pairs = (pair_up.at[0], pair_up.at[1], pair_c)
    kinds = (0, 0, 1, 1)
    spans = tuple(
        pl.ds((piece % 2) * (size // 2), size // 2)
        for piece, size in enumerate((width, width, model, model))
    )
    swaps = (swap_up, swap_down)
    fars = (far_up, far_down)
    lows = (low_up, low_down)
    theirs = (their_up, their_down)
    moments = (moment_up, moment_down)
    helds = (held_up, held_down)
    halves = (model // (2 * layers), width // (2 * layers))

    w_up_copy = pltpu.make_async_copy(up_hbm.at[core, 0], w_up, w_sem.at[0])
    w_down_copy = pltpu.make_async_copy(down_hbm.at[core, 0], w_down, w_sem.at[1])

    def aligned(start, size):
        return pl.ds(pl.multiple_of(start, size), size)

    def own_copy(slot):
        return pltpu.make_async_copy(
            inputs_hbm.at[core, 0, slot], x_buf.at[2 * slot + core], own_sem.at[slot]
        )

    def remote(src, dst, send, recv, device):
        return pltpu.make_async_remote_copy(
            src_ref=src, dst_ref=dst, send_sem=send, recv_sem=recv,
            device_id=device, device_id_type=MESH,
        )

    def swap_copy(slot):
        return remote(
            inputs_hbm.at[1 - core, 0, slot], x_buf.at[2 * slot + core],
            swap_send.at[slot], swap_recv.at[slot], (section, other),
        )

    def top_own(slot):
        return pltpu.make_async_copy(
            top_hbm.at[core, slot], e_buf.at[2 * slot + core], e_recv.at[2 * slot + core]
        )

    def top_swap(slot):
        return remote(
            top_hbm.at[1 - core, slot], e_buf.at[2 * slot + core],
            top_send.at[slot], e_recv.at[2 * slot + core], (section, other),
        )

    def relay_copy(chunk):
        return remote(
            sent.at[chunk], e_buf.at[chunk], e_send.at[chunk], e_recv.at[chunk], (after, replica)
        )

    def moment_copy(kind):
        return remote(
            lows[kind], theirs[kind], moment_send.at[kind], moment_recv.at[kind], (mirror, replica)
        )

    def ring_block(way, step):
        shift = layers - 1 - step if way == 0 else 1 + step
        return lax.rem(layer + shift, layers)

    def ring_rows(piece, way, step):
        half = halves[kinds[piece]]
        start = ring_block(way, step) * 2 * half
        if piece == 3:
            return aligned(start + side * half + way * (half // 2), half // 2)
        return aligned(start + way * half, half)

    def ring_copy(piece, way, step):
        return remote(
            parts[kinds[piece]].at[ring_rows(piece, way, step), spans[piece]],
            rings[piece].at[way, step],
            ring_send.at[piece, way, step], ring_recv.at[piece, way, step],
            (section, above if way == 0 else below),
        )

    def pair_copy(piece):
        half = halves[kinds[piece]]
        start = layer * 2 * half + (1 - side) * half
        return remote(
            parts[kinds[piece]].at[aligned(start, half), spans[piece]], pairs[piece],
            pair_send.at[piece], pair_recv.at[piece], (section, beside),
        )

    def early_copy(block):
        half = halves[1]
        start = block * 2 * half + (1 - side) * half
        return remote(
            part_down.at[aligned(start, half), spans[3]], pair_d.at[block],
            pair_send.at[3 + block], pair_recv.at[3 + block], (section, beside),
        )

    def final_rows(kind, which):
        half = halves[kind]
        quarter = half // 2
        return aligned(layer * 2 * half + side * half + which * quarter, quarter)

    def give_copies(piece):
        kind = kinds[piece]
        cols = spans[piece]
        return (
            remote(
                parts[kind].at[final_rows(kind, core), cols], fars[kind].at[0, :, cols],
                give_send.at[piece, 0], give_recv.at[piece, 0], (mirror, replica),
            ),
            remote(
                parts[kind].at[final_rows(kind, 1 - core), cols], fars[kind].at[1, :, cols],
                give_send.at[piece, 1], give_recv.at[piece, 1], (mirror, other),
            ),
            remote(
                parts[kind].at[final_rows(kind, 1 - core), cols], swaps[kind].at[:, cols],
                give_send.at[piece, 2], give_recv.at[piece, 2], (section, other),
            ),
        )

    state_copies = []
    for kind, (held_hbm, moment_hbm) in enumerate(
        ((up_hbm, moment_up_hbm), (down_hbm, moment_down_hbm))
    ):
        state_copies.append(
            pltpu.make_async_copy(moment_hbm.at[0], moments[kind], state_sem.at[kind, 0])
        )
        count = helds[kind].shape[1]
        for c in range(2):
            state_copies.append(
                pltpu.make_async_copy(
                    held_hbm.at[c, 0, aligned(replica * count, count), :],
                    helds[kind].at[c], state_sem.at[kind, 1 + c],
                )
            )

    w_up_copy.start()
    for slot in range(micro):
        own_copy(slot).start()
    w_down_copy.start()

    barrier = pltpu.get_barrier_semaphore()
    for device in (
        (after, replica), (before, replica), (section, other), (section, above),
        (section, below), (section, beside), (mirror, replica), (mirror, other),
    ):
        pl.semaphore_signal(barrier, inc=1, device_id=device, device_id_type=MESH)
    pl.semaphore_wait(barrier, 8)

    @pl.when(position == last)
    def _():
        for slot in range(micro):
            top_swap(slot).start()

    for slot in range(micro):
        swap_copy(slot).start()

    @pl.when(position == 0)
    def _():
        for slot in range(micro):
            top_own(slot).start()

    turned_down, turned_up = part_up, part_down
    across = min(256, model)

    w_up_copy.wait()

    @pl.loop(0, width // across)
    def _(t):
        cols = aligned(t * across, across)
        turned_up[cols, :] = w_up[:, cols].T

    w_down_copy.wait()

    @pl.loop(0, width // across)
    def _(t):
        cols = aligned(t * across, across)
        turned_down[:, cols] = w_down[cols, :].T

    for slot in range(micro):
        own_copy(slot).wait()
        swap_copy(slot).wait()
    for copy in state_copies:
        copy.start()

    def forward(chunk):
        x = x_buf[2 * plan_ref[core, chunk // 2] + lax.rem(chunk, 2)]
        x_plan[chunk] = x

        for n in range(width // tile):
            cols = pl.ds(n * tile, tile)
            preact = jnp.dot(x, w_up[:, cols], preferred_element_type=f32)
            cdf = 0.5 * (1.0 + lax.erf(preact * root_half))
            hidden[chunk, :, cols] = (preact * cdf).astype(bf16)
            grown = cdf + preact * jnp.exp(-0.5 * preact * preact) * inv_root_tau
            slope[chunk, :, cols] = grown.astype(bf16)
        summed = x.astype(f32) + jnp.dot(hidden[chunk], w_down[...], preferred_element_type=f32)
        centre = summed - jnp.mean(summed, axis=-1, keepdims=True)
        scale_inv = lax.rsqrt(jnp.mean(centre * centre, axis=-1, keepdims=True) + norm_epsilon)
        normed[chunk] = centre * scale_inv
        scale_buf[chunk] = jnp.broadcast_to(scale_inv, (rows, 128))

    def backward(chunk):
        pltpu.make_async_copy(sent.at[chunk], e_buf.at[chunk], e_recv.at[chunk]).wait()
        upstream = e_buf[chunk].astype(f32)
        y = normed[chunk]
        scale_inv = scale_buf[chunk][:, :1]
        grad_sum = scale_inv * (
            upstream
            - jnp.mean(upstream, axis=-1, keepdims=True)
            - y * jnp.mean(upstream * y, axis=-1, keepdims=True)
        )
        low = grad_sum.astype(bf16)
        place = aligned(chunk * rows, rows)
        grad_low[place, :] = low
        for n in range(width // tile):
            cols = pl.ds(n * tile, tile)
            grad = jnp.dot(low, turned_down[:, cols], preferred_element_type=f32)
            grad = grad * slope[chunk, :, cols].astype(f32)
            grad_pre[place, cols] = grad.astype(bf16)

        @pl.when(position < last)
        def _():
            grad_in = jnp.dot(grad_pre[place, :], turned_up[...], preferred_element_type=f32)
            sent[chunk] = (grad_sum + grad_in).astype(bf16)
            relay_copy(chunk).start()

    lead = jnp.minimum(chunks, ahead * position)

    @pl.loop(0, 2 * chunks)
    def _(step):
        @pl.when(step < chunks)
        def _():
            forward(step)

        back = step - lead

        @pl.when(jnp.logical_and(back >= 0, back < chunks))
        def _():
            backward(back)

        @pl.when(step == chunks - 1)
        def _():
            for copy in state_copies:
                copy.wait()
            for kind in range(2):
                lows[kind][...] = moments[kind][...].astype(bf16)
                moment_copy(kind).start()

    total = chunks * rows
    up_rows, down_rows = 2 * halves[0], halves[1]

    def up_block(block):
        cols = aligned(block * up_rows, up_rows)
        left = x_plan[:, :, cols].reshape(total, up_rows)
        part_up[cols, :] = contract_rows(left, grad_pre[...]).astype(bf16)

    def down_block(block, which):
        cols = aligned(block * 2 * down_rows + which * down_rows, down_rows)
        left = hidden[:, :, cols].reshape(total, down_rows)
        part_down[cols, :] = contract_rows(left, grad_low[...]).astype(bf16)

    def add_rows(piece, place, value):
        part = parts[kinds[piece]]
        cols = spans[piece]
        part[place, cols] = (part[place, cols].astype(f32) + value.astype(f32)).astype(bf16)

    def turn(piece, step):
        for way in range(2):
            ring_copy(piece, way, step).wait_recv()
            add_rows(piece, ring_rows(piece, way, step + 1), rings[piece][way, step])
            if step < layers - 2:
                ring_copy(piece, way, step + 1).start()

    def give(piece):
        for copy in give_copies(piece):
            copy.start()

    def settle(piece):
        half = halves[kinds[piece]]
        pair_copy(piece).wait_recv()
        add_rows(piece, aligned(layer * 2 * half + side * half, half), pairs[piece][...])
        give(piece)

    def update(kind, out, out_moment):
        for piece in (2 * kind, 2 * kind + 1):
            for copy in give_copies(piece):
                copy.wait_recv()
        own = parts[kind][final_rows(kind, core), :].astype(f32)
        got = swaps[kind][...].astype(f32)
        same = fars[kind][0].astype(f32)
        cross = fars[kind][1].astype(f32)
        zero = core == 0
        grad = jnp.where(zero, own + cross, got + same)
        grad_mirror = jnp.where(zero, got + same, own + cross)
        moment = momentum_decay * moments[kind][...] + grad
        out_moment[...] = moment
        out[0] = (helds[kind][0].astype(f32) - step_size * moment).astype(bf16)
        mirrored = momentum_decay * theirs[kind][...].astype(f32) + grad_mirror
        out[1] = (helds[kind][1].astype(f32) - step_size * mirrored).astype(bf16)

    order = (layers - 1, 1, 2, 0)

    @pl.loop(0, 2)
    def _(i):
        up_block(lax.rem(layer + jnp.where(i == 0, order[0], order[1]), layers))

        @pl.when(i == 0)
        def _():
            ring_copy(0, 0, 0).start()
            ring_copy(1, 0, 0).start()

        @pl.when(i == 1)
        def _():
            ring_copy(0, 1, 0).start()
            ring_copy(1, 1, 0).start()

    def place(shift):
        return lax.rem(layer + shift, layers)

    def down_early(shift):
        down_block(place(shift), 1 - side)
        early_copy(place(shift)).start()

    @pl.loop(0, 2)
    def _(i):
        down_early(jnp.where(i == 0, order[0], order[1]))

    up_block(place(order[2]))
    down_early(order[2])
    turn(0, 0)
    turn(1, 0)
    down_early(order[3])
    up_block(place(order[3]))

    @pl.loop(0, 2)
    def _(i):
        down_block(place(jnp.where(i == 0, order[0], order[1])), side)

    turn(0, 1)
    turn(1, 1)
    for way in range(2):
        ring_copy(2, way, 0).start()

    @pl.loop(0, 2)
    def _(i):
        down_block(place(jnp.where(i == 0, order[2], order[3])), side)

    turn(0, 2)
    pair_copy(0).start()
    turn(1, 2)
    pair_copy(1).start()

    @pl.loop(0, layers)
    def _(block):
        early_copy(block).wait_recv()
        add_rows(3, aligned(block * 2 * down_rows + side * down_rows, down_rows), pair_d[block])

    for way in range(2):
        ring_copy(3, way, 0).start()
    settle(0)
    turn(2, 0)
    settle(1)
    turn(3, 0)
    turn(2, 1)
    turn(3, 1)
    turn(2, 2)
    pair_copy(2).start()
    turn(3, 2)
    give(3)
    settle(2)
    for kind in range(2):
        moment_copy(kind).wait()
    update(0, new_up, new_moment_up)
    update(1, new_down, new_moment_down)

    for piece in range(4):
        for way in range(2):
            for step in range(layers - 1):
                ring_copy(piece, way, step).wait_send()
        for copy in give_copies(piece):
            copy.wait_send()
    for piece in range(3):
        pair_copy(piece).wait_send()
    for block in range(layers):
        early_copy(block).wait_send()

    @pl.when(position < last)
    def _():
        for chunk in range(chunks):
            relay_copy(chunk).wait_send()

    @pl.when(position == last)
    def _():
        for slot in range(micro):
            top_swap(slot).wait_send()


def relay(sections, replicas, plan, inputs, top_grad, up_weight, down_weight, up_moment, down_moment):
    micro, rows, model = inputs.shape[2:]
    width = up_weight.shape[3]
    chunks = 2 * micro
    total = chunks * rows
    layers = replicas // 4
    half_up, half_down = model // (2 * layers), width // (2 * layers)
    held_up, held_down = half_up // 2, half_down // 2
    dma = pltpu.SemaphoreType.DMA
    flops = 2 * 6 * total * model * width
    return pl.pallas_call(
        functools.partial(
            relay_kernel, sections, replicas, micro, rows, model, width, min(512, width), 3
        ),
        out_shape=[
            jax.ShapeDtypeStruct((2, held_up, width), bf16),
            jax.ShapeDtypeStruct((2, held_down, model), bf16),
            jax.ShapeDtypeStruct((held_up, width), f32),
            jax.ShapeDtypeStruct((held_down, model), f32),
        ],
        in_specs=[pl.BlockSpec(memory_space=pltpu.SMEM)] + [pl.BlockSpec(memory_space=pl.ANY)] * 6,
        out_specs=[pl.BlockSpec(memory_space=pltpu.VMEM)] * 4,
        scratch_shapes=[
            pltpu.VMEM((model, width), bf16),
            pltpu.VMEM((width, model), bf16),
            pltpu.VMEM((chunks, rows, model), bf16),
            pltpu.VMEM((chunks, rows, model), bf16),
            pltpu.VMEM((chunks, rows, width), bf16),
            pltpu.VMEM((chunks, rows, width), bf16),
            pltpu.VMEM((chunks, rows, model), f32),
            pltpu.VMEM((chunks, rows, 128), f32),
            pltpu.VMEM((total, width), bf16),
            pltpu.VMEM((total, model), bf16),
            pltpu.VMEM((chunks, rows, model), bf16),
            pltpu.VMEM((chunks, rows, model), bf16),
            pltpu.VMEM((model, width), bf16),
            pltpu.VMEM((width, model), bf16),
            pltpu.VMEM((2, 2, layers - 1, half_up, width // 2), bf16),
            pltpu.VMEM((2, layers - 1, half_down, model // 2), bf16),
            pltpu.VMEM((2, layers - 1, half_down // 2, model // 2), bf16),
            pltpu.VMEM((2, half_up, width // 2), bf16),
            pltpu.VMEM((half_down, model // 2), bf16),
            pltpu.VMEM((layers, half_down, model // 2), bf16),
            pltpu.VMEM((held_up, width), bf16),
            pltpu.VMEM((held_down, model), bf16),
            pltpu.VMEM((2, held_up, width), bf16),
            pltpu.VMEM((2, held_down, model), bf16),
            pltpu.VMEM((held_up, width), f32),
            pltpu.VMEM((held_down, model), f32),
            pltpu.VMEM((held_up, width), bf16),
            pltpu.VMEM((held_down, model), bf16),
            pltpu.VMEM((held_up, width), bf16),
            pltpu.VMEM((held_down, model), bf16),
            pltpu.VMEM((2, held_up, width), bf16),
            pltpu.VMEM((2, held_down, model), bf16),
            dma((2,)),
            dma((micro,)),
            dma((micro,)),
            dma((micro,)),
            dma((micro,)),
            dma((chunks,)),
            dma((chunks,)),
            dma((2, 3)),
            dma((2,)),
            dma((2,)),
            dma((4, 2, layers - 1)),
            dma((4, 2, layers - 1)),
            dma((3 + layers,)),
            dma((3 + layers,)),
            dma((4, 3)),
            dma((4, 3)),
        ],
        compiler_params=pltpu.CompilerParams(
            collective_id=0, has_side_effects=True, vmem_limit_bytes=60 * 1024 * 1024
        ),
        cost_estimate=pl.CostEstimate(flops=flops, bytes_accessed=24 << 20, transcendentals=0),
    )(plan, inputs, top_grad, up_weight, down_weight, up_moment, down_moment)


def hand_on_kernel(count, *refs):
    sources, targets = refs[:count], refs[count:2 * count]
    staged, load_sem, store_sem = refs[2 * count:3 * count], refs[3 * count], refs[3 * count + 1]
    loads = []
    stores = []
    for i in range(count):
        half = sources[i].shape[0] // 2
        for j in range(2):
            rows = pl.ds(j * half, half)
            loads.append(pltpu.make_async_copy(
                sources[i].at[rows], staged[i].at[rows], load_sem.at[i, j]
            ))
            stores.append(pltpu.make_async_copy(
                staged[i].at[rows], targets[i].at[rows], store_sem.at[i, j]
            ))
    for load in loads:
        load.start()
    for load, store in zip(loads, stores):
        load.wait()
        store.start()
    for store in stores:
        store.wait()


def hand_on(*values):
    count = len(values)
    return pl.pallas_call(
        functools.partial(hand_on_kernel, count),
        out_shape=[jax.ShapeDtypeStruct(v.shape, v.dtype) for v in values],
        in_specs=[pl.BlockSpec(memory_space=pl.ANY)] * count,
        out_specs=[pl.BlockSpec(memory_space=pl.ANY)] * count,
        scratch_shapes=[pltpu.VMEM(v.shape, v.dtype) for v in values]
        + [pltpu.SemaphoreType.DMA((count, 2))] * 2,
        compiler_params=pltpu.CompilerParams(vmem_limit_bytes=60 * 1024 * 1024),
    )(*values)


def on_device(section_inputs, top_grad, plan, up_weight, down_weight, up_moment, down_moment):
    new_up, new_down, moment_up, moment_down = hand_on(*relay(
        lax.axis_size("section"), lax.axis_size("dp"), plan, section_inputs,
        top_grad, up_weight, down_weight, up_moment, down_moment,
    ))
    return (new_up[:, None], new_down[:, None], moment_up[None], moment_down[None])


def solution(mesh):
    in_specs = (
        P(None, "section", None, "dp", None),
        P(None, None, "dp", None),
        P(),
        P(None, "section", None, None),
        P(None, "section", None, None),
        P("section", "dp", None),
        P("section", "dp", None),
    )
    out_specs = (
        P(None, "section", "dp", None),
        P(None, "section", "dp", None),
        P("section", "dp", None),
        P("section", "dp", None),
    )
    return jax.shard_map(
        on_device, mesh=mesh, in_specs=in_specs, out_specs=out_specs, check_vma=False
    )
```

```python
import functools

import jax
import jax.numpy as jnp
from jax import lax
from jax.experimental import pallas as pl
from jax.experimental.pallas import tpu as pltpu
from jax.sharding import PartitionSpec as P

norm_epsilon = 1e-06
momentum_decay = 0.9
step_size = 0.01
root_half = 0.7071067811865476
inv_root_tau = 0.3989422804014327
MESH = pl.DeviceIdType.MESH
bf16 = jnp.bfloat16
f32 = jnp.float32


def contract_rows(left, right):
    return lax.dot_general(
        left, right, (((0,), (0,)), ((), ())), preferred_element_type=f32
    )


def relay_kernel(
    sections, replicas, micro, rows, model, width, tile, ahead,
    plan_ref, inputs_hbm, top_hbm, up_hbm, down_hbm, moment_up_hbm, moment_down_hbm,
    new_up, new_down, new_moment_up, new_moment_down,
    w_up, w_down, x_buf, x_plan, hidden, slope, normed, scale_buf, grad_pre, grad_low, e_buf, sent,
    part_up, part_down, ring_up, ring_c, ring_d, pair_up, pair_c, pair_d, swap_up, swap_down,
    far_up, far_down, moment_up, moment_down, low_up, low_down, their_up, their_down,
    held_up, held_down,
    w_sem, own_sem, swap_send, swap_recv, top_send, e_recv, e_send,
    state_sem, moment_send, moment_recv, ring_send, ring_recv, pair_send, pair_recv,
    give_send, give_recv,
):
    section = lax.axis_index("section")
    replica = lax.axis_index("dp")
    core = lax.rem(replica, 2)
    other = replica + 1 - 2 * core
    side = lax.rem(replica // 2, 2)
    layer = replica // 4
    layers = replicas // 4
    above = lax.rem(replica + 4, replicas)
    below = lax.rem(replica + replicas - 4, replicas)
    beside = replica + 2 - 4 * side
    mirror = sections - 1 - section
    position = jnp.where(core == 0, sections - 1 - section, section)
    step_to = 2 * core - 1
    after = lax.rem(section + step_to + sections, sections)
    before = lax.rem(section - step_to + sections, sections)
    chunks = 2 * micro
    last = sections - 1
    parts = (part_up, part_down)
    rings = (ring_up.at[0], ring_up.at[1], ring_c, ring_d)
    pairs = (pair_up.at[0], pair_up.at[1], pair_c)
    kinds = (0, 0, 1, 1)
    spans = tuple(
        pl.ds((piece % 2) * (size // 2), size // 2)
        for piece, size in enumerate((width, width, model, model))
    )
    swaps = (swap_up, swap_down)
    fars = (far_up, far_down)
    lows = (low_up, low_down)
    theirs = (their_up, their_down)
    moments = (moment_up, moment_down)
    helds = (held_up, held_down)
    halves = (model // (2 * layers), width // (2 * layers))

    w_up_copy = pltpu.make_async_copy(up_hbm.at[core, 0], w_up, w_sem.at[0])
    w_down_copy = pltpu.make_async_copy(down_hbm.at[core, 0], w_down, w_sem.at[1])

    def aligned(start, size):
        return pl.ds(pl.multiple_of(start, size), size)

    def own_copy(slot):
        return pltpu.make_async_copy(
            inputs_hbm.at[core, 0, slot], x_buf.at[2 * slot + core], own_sem.at[slot]
        )

    def remote(src, dst, send, recv, device):
        return pltpu.make_async_remote_copy(
            src_ref=src, dst_ref=dst, send_sem=send, recv_sem=recv,
            device_id=device, device_id_type=MESH,
        )

    def swap_copy(slot):
        return remote(
            inputs_hbm.at[1 - core, 0, slot], x_buf.at[2 * slot + core],
            swap_send.at[slot], swap_recv.at[slot], (section, other),
        )

    def top_own(slot):
        return pltpu.make_async_copy(
            top_hbm.at[core, slot], e_buf.at[2 * slot + core], e_recv.at[2 * slot + core]
        )

    def top_swap(slot):
        return remote(
            top_hbm.at[1 - core, slot], e_buf.at[2 * slot + core],
            top_send.at[slot], e_recv.at[2 * slot + core], (section, other),
        )

    def relay_copy(chunk):
        return remote(
            sent.at[chunk], e_buf.at[chunk], e_send.at[chunk], e_recv.at[chunk], (after, replica)
        )

    def moment_copy(kind):
        return remote(
            lows[kind], theirs[kind], moment_send.at[kind], moment_recv.at[kind], (mirror, replica)
        )

    def ring_block(way, step):
        shift = layers - 1 - step if way == 0 else 1 + step
        return lax.rem(layer + shift, layers)

    def ring_rows(piece, way, step):
        half = halves[kinds[piece]]
        start = ring_block(way, step) * 2 * half
        if piece == 3:
            return aligned(start + side * half + way * (half // 2), half // 2)
        return aligned(start + way * half, half)

    def ring_copy(piece, way, step):
        return remote(
            parts[kinds[piece]].at[ring_rows(piece, way, step), spans[piece]],
            rings[piece].at[way, step],
            ring_send.at[piece, way, step], ring_recv.at[piece, way, step],
            (section, above if way == 0 else below),
        )

    def pair_copy(piece):
        half = halves[kinds[piece]]
        start = layer * 2 * half + (1 - side) * half
        return remote(
            parts[kinds[piece]].at[aligned(start, half), spans[piece]], pairs[piece],
            pair_send.at[piece], pair_recv.at[piece], (section, beside),
        )

    def early_copy(block):
        half = halves[1]
        start = block * 2 * half + (1 - side) * half
        return remote(
            part_down.at[aligned(start, half), spans[3]], pair_d.at[block],
            pair_send.at[3 + block], pair_recv.at[3 + block], (section, beside),
        )

    def final_rows(kind, which):
        half = halves[kind]
        quarter = half // 2
        return aligned(layer * 2 * half + side * half + which * quarter, quarter)

    def give_copies(piece):
        kind = kinds[piece]
        cols = spans[piece]
        return (
            remote(
                parts[kind].at[final_rows(kind, core), cols], fars[kind].at[0, :, cols],
                give_send.at[piece, 0], give_recv.at[piece, 0], (mirror, replica),
            ),
            remote(
                parts[kind].at[final_rows(kind, 1 - core), cols], fars[kind].at[1, :, cols],
                give_send.at[piece, 1], give_recv.at[piece, 1], (mirror, other),
            ),
            remote(
                parts[kind].at[final_rows(kind, 1 - core), cols], swaps[kind].at[:, cols],
                give_send.at[piece, 2], give_recv.at[piece, 2], (section, other),
            ),
        )

    state_copies = []
    for kind, (held_hbm, moment_hbm) in enumerate(
        ((up_hbm, moment_up_hbm), (down_hbm, moment_down_hbm))
    ):
        state_copies.append(
            pltpu.make_async_copy(moment_hbm.at[0], moments[kind], state_sem.at[kind, 0])
        )
        count = helds[kind].shape[1]
        for c in range(2):
            state_copies.append(
                pltpu.make_async_copy(
                    held_hbm.at[c, 0, aligned(replica * count, count), :],
                    helds[kind].at[c], state_sem.at[kind, 1 + c],
                )
            )

    w_up_copy.start()
    for slot in range(micro):
        own_copy(slot).start()
    w_down_copy.start()

    for copy in state_copies:
        copy.start()

    barrier = pltpu.get_barrier_semaphore()
    for device in (
        (after, replica), (before, replica), (section, other), (section, above),
        (section, below), (section, beside), (mirror, replica), (mirror, other),
    ):
        pl.semaphore_signal(barrier, inc=1, device_id=device, device_id_type=MESH)
    pl.semaphore_wait(barrier, 8)

    @pl.when(position == last)
    def _():
        for slot in range(micro):
            top_swap(slot).start()

    for slot in range(micro):
        swap_copy(slot).start()

    @pl.when(position == 0)
    def _():
        for slot in range(micro):
            top_own(slot).start()

    turned_down, turned_up = part_up, part_down
    across = min(256, model)

    def send_moments():
        for kind in range(2):
            moment_copy(kind).start()

    w_up_copy.wait()

    @pl.loop(0, width // across)
    def _(t):
        cols = aligned(t * across, across)
        turned_up[cols, :] = w_up[:, cols].T

    w_down_copy.wait()

    @pl.loop(0, width // across)
    def _(t):
        cols = aligned(t * across, across)
        turned_down[:, cols] = w_down[cols, :].T

    for copy in state_copies:
        copy.wait()
    for kind in range(2):
        lows[kind][...] = moments[kind][...].astype(bf16)

    @pl.when(position > 0)
    def _():
        send_moments()

    for slot in range(micro):
        own_copy(slot).wait()
        swap_copy(slot).wait()

    def forward(chunk):
        x = x_buf[2 * plan_ref[core, chunk // 2] + lax.rem(chunk, 2)]
        x_plan[chunk] = x

        for n in range(width // tile):
            cols = pl.ds(n * tile, tile)
            preact = jnp.dot(x, w_up[:, cols], preferred_element_type=f32)
            cdf = 0.5 * (1.0 + lax.erf(preact * root_half))
            hidden[chunk, :, cols] = (preact * cdf).astype(bf16)
            grown = cdf + preact * jnp.exp(-0.5 * preact * preact) * inv_root_tau
            slope[chunk, :, cols] = grown.astype(bf16)
        summed = x.astype(f32) + jnp.dot(hidden[chunk], w_down[...], preferred_element_type=f32)
        centre = summed - jnp.mean(summed, axis=-1, keepdims=True)
        scale_inv = lax.rsqrt(jnp.mean(centre * centre, axis=-1, keepdims=True) + norm_epsilon)
        normed[chunk] = centre * scale_inv
        scale_buf[chunk] = jnp.broadcast_to(scale_inv, (rows, 128))

    def backward(chunk):
        pltpu.make_async_copy(sent.at[chunk], e_buf.at[chunk], e_recv.at[chunk]).wait()
        upstream = e_buf[chunk].astype(f32)
        y = normed[chunk]
        scale_inv = scale_buf[chunk][:, :1]
        grad_sum = scale_inv * (
            upstream
            - jnp.mean(upstream, axis=-1, keepdims=True)
            - y * jnp.mean(upstream * y, axis=-1, keepdims=True)
        )
        low = grad_sum.astype(bf16)
        place = aligned(chunk * rows, rows)
        grad_low[place, :] = low
        for n in range(width // tile):
            cols = pl.ds(n * tile, tile)
            grad = jnp.dot(low, turned_down[:, cols], preferred_element_type=f32)
            grad = grad * slope[chunk, :, cols].astype(f32)
            grad_pre[place, cols] = grad.astype(bf16)

        @pl.when(position < last)
        def _():
            grad_in = jnp.dot(grad_pre[place, :], turned_up[...], preferred_element_type=f32)
            sent[chunk] = (grad_sum + grad_in).astype(bf16)
            relay_copy(chunk).start()

    lead = jnp.minimum(chunks, ahead * position)

    @pl.loop(0, 2 * chunks)
    def _(step):
        @pl.when(step < chunks)
        def _():
            forward(step)

        back = step - lead

        @pl.when(jnp.logical_and(back >= 0, back < chunks))
        def _():
            backward(back)

    total = chunks * rows
    up_rows, down_rows = 2 * halves[0], halves[1]

    def up_block(block):
        cols = aligned(block * up_rows, up_rows)
        left = x_plan[:, :, cols].reshape(total, up_rows)
        part_up[cols, :] = contract_rows(left, grad_pre[...]).astype(bf16)

    def down_block(block, which):
        cols = aligned(block * 2 * down_rows + which * down_rows, down_rows)
        left = hidden[:, :, cols].reshape(total, down_rows)
        part_down[cols, :] = contract_rows(left, grad_low[...]).astype(bf16)

    def add_rows(piece, place, value):
        part = parts[kinds[piece]]
        cols = spans[piece]
        part[place, cols] = (part[place, cols].astype(f32) + value.astype(f32)).astype(bf16)

    def turn(piece, step):
        for way in range(2):
            ring_copy(piece, way, step).wait_recv()
            add_rows(piece, ring_rows(piece, way, step + 1), rings[piece][way, step])
            if step < layers - 2:
                ring_copy(piece, way, step + 1).start()

    def give(piece):
        for copy in give_copies(piece):
            copy.start()

    def settle(piece):
        half = halves[kinds[piece]]
        pair_copy(piece).wait_recv()
        add_rows(piece, aligned(layer * 2 * half + side * half, half), pairs[piece][...])
        give(piece)

    def update(kind, out, out_moment):
        for piece in (2 * kind, 2 * kind + 1):
            for copy in give_copies(piece):
                copy.wait_recv()
        own = parts[kind][final_rows(kind, core), :].astype(f32)
        got = swaps[kind][...].astype(f32)
        same = fars[kind][0].astype(f32)
        cross = fars[kind][1].astype(f32)
        zero = core == 0
        grad = jnp.where(zero, own + cross, got + same)
        grad_mirror = jnp.where(zero, got + same, own + cross)
        moment = momentum_decay * moments[kind][...] + grad
        out_moment[...] = moment
        out[0] = (helds[kind][0].astype(f32) - step_size * moment).astype(bf16)
        mirrored = momentum_decay * theirs[kind][...].astype(f32) + grad_mirror
        out[1] = (helds[kind][1].astype(f32) - step_size * mirrored).astype(bf16)

    order = (layers - 1, 1, 2, 0)

    @pl.loop(0, 2)
    def _(i):
        up_block(lax.rem(layer + jnp.where(i == 0, order[0], order[1]), layers))

        @pl.when(i == 0)
        def _():
            ring_copy(0, 0, 0).start()
            ring_copy(1, 0, 0).start()

        @pl.when(i == 1)
        def _():
            ring_copy(0, 1, 0).start()
            ring_copy(1, 1, 0).start()

    def place(shift):
        return lax.rem(layer + shift, layers)

    def down_early(shift):
        down_block(place(shift), 1 - side)
        early_copy(place(shift)).start()

    @pl.loop(0, 2)
    def _(i):
        down_early(jnp.where(i == 0, order[0], order[1]))

    up_block(place(order[2]))
    down_early(order[2])
    turn(0, 0)
    turn(1, 0)
    down_early(order[3])
    up_block(place(order[3]))

    @pl.loop(0, 2)
    def _(i):
        down_block(place(jnp.where(i == 0, order[0], order[1])), side)

    turn(0, 1)
    turn(1, 1)
    for way in range(2):
        ring_copy(2, way, 0).start()

    @pl.loop(0, 2)
    def _(i):
        down_block(place(jnp.where(i == 0, order[2], order[3])), side)

    turn(0, 2)
    pair_copy(0).start()
    turn(1, 2)
    pair_copy(1).start()

    @pl.loop(0, layers)
    def _(block):
        early_copy(block).wait_recv()
        add_rows(3, aligned(block * 2 * down_rows + side * down_rows, down_rows), pair_d[block])

    for way in range(2):
        ring_copy(3, way, 0).start()
    settle(0)
    turn(2, 0)
    settle(1)
    turn(3, 0)
    turn(2, 1)
    turn(3, 1)
    turn(2, 2)
    pair_copy(2).start()
    turn(3, 2)
    give(3)

    @pl.when(position == 0)
    def _():
        send_moments()

    settle(2)
    for kind in range(2):
        moment_copy(kind).wait()
    update(0, new_up, new_moment_up)
    update(1, new_down, new_moment_down)

    for piece in range(4):
        for way in range(2):
            for step in range(layers - 1):
                ring_copy(piece, way, step).wait_send()
        for copy in give_copies(piece):
            copy.wait_send()
    for piece in range(3):
        pair_copy(piece).wait_send()
    for block in range(layers):
        early_copy(block).wait_send()

    @pl.when(position < last)
    def _():
        for chunk in range(chunks):
            relay_copy(chunk).wait_send()

    @pl.when(position == last)
    def _():
        for slot in range(micro):
            top_swap(slot).wait_send()


def relay(sections, replicas, plan, inputs, top_grad, up_weight, down_weight, up_moment, down_moment):
    micro, rows, model = inputs.shape[2:]
    width = up_weight.shape[3]
    chunks = 2 * micro
    total = chunks * rows
    layers = replicas // 4
    half_up, half_down = model // (2 * layers), width // (2 * layers)
    held_up, held_down = half_up // 2, half_down // 2
    dma = pltpu.SemaphoreType.DMA
    flops = 2 * 6 * total * model * width
    return pl.pallas_call(
        functools.partial(
            relay_kernel, sections, replicas, micro, rows, model, width, min(512, width), 3
        ),
        out_shape=[
            jax.ShapeDtypeStruct((2, held_up, width), bf16),
            jax.ShapeDtypeStruct((2, held_down, model), bf16),
            jax.ShapeDtypeStruct((held_up, width), f32),
            jax.ShapeDtypeStruct((held_down, model), f32),
        ],
        in_specs=[pl.BlockSpec(memory_space=pltpu.SMEM)] + [pl.BlockSpec(memory_space=pl.ANY)] * 6,
        out_specs=[pl.BlockSpec(memory_space=pltpu.VMEM)] * 4,
        scratch_shapes=[
            pltpu.VMEM((model, width), bf16),
            pltpu.VMEM((width, model), bf16),
            pltpu.VMEM((chunks, rows, model), bf16),
            pltpu.VMEM((chunks, rows, model), bf16),
            pltpu.VMEM((chunks, rows, width), bf16),
            pltpu.VMEM((chunks, rows, width), bf16),
            pltpu.VMEM((chunks, rows, model), f32),
            pltpu.VMEM((chunks, rows, 128), f32),
            pltpu.VMEM((total, width), bf16),
            pltpu.VMEM((total, model), bf16),
            pltpu.VMEM((chunks, rows, model), bf16),
            pltpu.VMEM((chunks, rows, model), bf16),
            pltpu.VMEM((model, width), bf16),
            pltpu.VMEM((width, model), bf16),
            pltpu.VMEM((2, 2, layers - 1, half_up, width // 2), bf16),
            pltpu.VMEM((2, layers - 1, half_down, model // 2), bf16),
            pltpu.VMEM((2, layers - 1, half_down // 2, model // 2), bf16),
            pltpu.VMEM((2, half_up, width // 2), bf16),
            pltpu.VMEM((half_down, model // 2), bf16),
            pltpu.VMEM((layers, half_down, model // 2), bf16),
            pltpu.VMEM((held_up, width), bf16),
            pltpu.VMEM((held_down, model), bf16),
            pltpu.VMEM((2, held_up, width), bf16),
            pltpu.VMEM((2, held_down, model), bf16),
            pltpu.VMEM((held_up, width), f32),
            pltpu.VMEM((held_down, model), f32),
            pltpu.VMEM((held_up, width), bf16),
            pltpu.VMEM((held_down, model), bf16),
            pltpu.VMEM((held_up, width), bf16),
            pltpu.VMEM((held_down, model), bf16),
            pltpu.VMEM((2, held_up, width), bf16),
            pltpu.VMEM((2, held_down, model), bf16),
            dma((2,)),
            dma((micro,)),
            dma((micro,)),
            dma((micro,)),
            dma((micro,)),
            dma((chunks,)),
            dma((chunks,)),
            dma((2, 3)),
            dma((2,)),
            dma((2,)),
            dma((4, 2, layers - 1)),
            dma((4, 2, layers - 1)),
            dma((3 + layers,)),
            dma((3 + layers,)),
            dma((4, 3)),
            dma((4, 3)),
        ],
        compiler_params=pltpu.CompilerParams(
            collective_id=0, has_side_effects=True, vmem_limit_bytes=60 * 1024 * 1024
        ),
        cost_estimate=pl.CostEstimate(flops=flops, bytes_accessed=24 << 20, transcendentals=0),
    )(plan, inputs, top_grad, up_weight, down_weight, up_moment, down_moment)


def hand_on_kernel(count, *refs):
    sources, targets = refs[:count], refs[count:2 * count]
    staged, load_sem, store_sem = refs[2 * count:3 * count], refs[3 * count], refs[3 * count + 1]
    loads = []
    stores = []
    for i in range(count):
        half = sources[i].shape[0] // 2
        for j in range(2):
            rows = pl.ds(j * half, half)
            loads.append(pltpu.make_async_copy(
                sources[i].at[rows], staged[i].at[rows], load_sem.at[i, j]
            ))
            stores.append(pltpu.make_async_copy(
                staged[i].at[rows], targets[i].at[rows], store_sem.at[i, j]
            ))
    for load in loads:
        load.start()
    for load, store in zip(loads, stores):
        load.wait()
        store.start()
    for store in stores:
        store.wait()


def hand_on(*values):
    count = len(values)
    return pl.pallas_call(
        functools.partial(hand_on_kernel, count),
        out_shape=[jax.ShapeDtypeStruct(v.shape, v.dtype) for v in values],
        in_specs=[pl.BlockSpec(memory_space=pl.ANY)] * count,
        out_specs=[pl.BlockSpec(memory_space=pl.ANY)] * count,
        scratch_shapes=[pltpu.VMEM(v.shape, v.dtype) for v in values]
        + [pltpu.SemaphoreType.DMA((count, 2))] * 2,
        compiler_params=pltpu.CompilerParams(vmem_limit_bytes=60 * 1024 * 1024),
    )(*values)


def on_device(section_inputs, top_grad, plan, up_weight, down_weight, up_moment, down_moment):
    new_up, new_down, moment_up, moment_down = hand_on(*relay(
        lax.axis_size("section"), lax.axis_size("dp"), plan, section_inputs,
        top_grad, up_weight, down_weight, up_moment, down_moment,
    ))
    return (new_up[:, None], new_down[:, None], moment_up[None], moment_down[None])


def solution(mesh):
    in_specs = (
        P(None, "section", None, "dp", None),
        P(None, None, "dp", None),
        P(),
        P(None, "section", None, None),
        P(None, "section", None, None),
        P("section", "dp", None),
        P("section", "dp", None),
    )
    out_specs = (
        P(None, "section", "dp", None),
        P(None, "section", "dp", None),
        P("section", "dp", None),
        P("section", "dp", None),
    )
    return jax.shard_map(
        on_device, mesh=mesh, in_specs=in_specs, out_specs=out_specs, check_vma=False
    )
```

```python
import functools

import jax
import jax.numpy as jnp
from jax import lax
from jax.experimental import pallas as pl
from jax.experimental.pallas import tpu as pltpu
from jax.sharding import PartitionSpec as P

norm_epsilon = 1e-06
momentum_decay = 0.9
step_size = 0.01
root_half = 0.7071067811865476
inv_root_tau = 0.3989422804014327
MESH = pl.DeviceIdType.MESH
bf16 = jnp.bfloat16
f32 = jnp.float32


def contract_rows(left, right):
    return lax.dot_general(
        left, right, (((0,), (0,)), ((), ())), preferred_element_type=f32
    )


def relay_kernel(
    sections, replicas, micro, rows, model, width, tile, ahead,
    plan_ref, inputs_hbm, top_hbm, up_hbm, down_hbm, moment_up_hbm, moment_down_hbm,
    new_up, new_down, new_moment_up, new_moment_down,
    w_up, w_down, x_buf, x_plan, hidden, slope, normed, scale_buf, grad_pre, grad_low, e_buf, sent,
    part_up, part_down, ring_up, ring_c, ring_d, pair_up, pair_c, pair_d, swap_up, swap_down,
    far_up, far_down, moment_up, moment_down, low_up, low_down, their_up, their_down,
    held_up, held_down,
    w_sem, own_sem, swap_send, swap_recv, top_send, e_recv, e_send,
    state_sem, moment_send, moment_recv, ring_send, ring_recv, pair_send, pair_recv,
    give_send, give_recv,
):
    section = lax.axis_index("section")
    replica = lax.axis_index("dp")
    core = lax.rem(replica, 2)
    other = replica + 1 - 2 * core
    side = lax.rem(replica // 2, 2)
    layer = replica // 4
    layers = replicas // 4
    above = lax.rem(replica + 4, replicas)
    below = lax.rem(replica + replicas - 4, replicas)
    beside = replica + 2 - 4 * side
    mirror = sections - 1 - section
    position = jnp.where(core == 0, sections - 1 - section, section)
    step_to = 2 * core - 1
    after = lax.rem(section + step_to + sections, sections)
    before = lax.rem(section - step_to + sections, sections)
    chunks = 2 * micro
    last = sections - 1
    parts = (part_up, part_down)
    rings = (ring_up.at[0], ring_up.at[1], ring_c, ring_d)
    pairs = (pair_up.at[0], pair_up.at[1], pair_c)
    kinds = (0, 0, 1, 1)
    cut = ring_c.shape[-1]
    spans = (
        pl.ds(0, width // 2), pl.ds(width // 2, width // 2),
        pl.ds(0, cut), pl.ds(cut, model - cut),
    )
    swaps = (swap_up, swap_down)
    fars = (far_up, far_down)
    lows = (low_up, low_down)
    theirs = (their_up, their_down)
    moments = (moment_up, moment_down)
    helds = (held_up, held_down)
    halves = (model // (2 * layers), width // (2 * layers))

    w_up_copy = pltpu.make_async_copy(up_hbm.at[core, 0], w_up, w_sem.at[0])
    w_down_copy = pltpu.make_async_copy(down_hbm.at[core, 0], w_down, w_sem.at[1])

    def aligned(start, size):
        return pl.ds(pl.multiple_of(start, size), size)

    def own_copy(slot):
        return pltpu.make_async_copy(
            inputs_hbm.at[core, 0, slot], x_buf.at[2 * slot + core], own_sem.at[slot]
        )

    def remote(src, dst, send, recv, device):
        return pltpu.make_async_remote_copy(
            src_ref=src, dst_ref=dst, send_sem=send, recv_sem=recv,
            device_id=device, device_id_type=MESH,
        )

    def swap_copy(slot):
        return remote(
            inputs_hbm.at[1 - core, 0, slot], x_buf.at[2 * slot + core],
            swap_send.at[slot], swap_recv.at[slot], (section, other),
        )

    def top_own(slot):
        return pltpu.make_async_copy(
            top_hbm.at[core, slot], e_buf.at[2 * slot + core], e_recv.at[2 * slot + core]
        )

    def top_swap(slot):
        return remote(
            top_hbm.at[1 - core, slot], e_buf.at[2 * slot + core],
            top_send.at[slot], e_recv.at[2 * slot + core], (section, other),
        )

    def relay_copy(chunk):
        return remote(
            sent.at[chunk], e_buf.at[chunk], e_send.at[chunk], e_recv.at[chunk], (after, replica)
        )

    def moment_copy(kind):
        return remote(
            lows[kind], theirs[kind], moment_send.at[kind], moment_recv.at[kind], (mirror, replica)
        )

    def ring_block(way, step):
        shift = layers - 1 - step if way == 0 else 1 + step
        return lax.rem(layer + shift, layers)

    def ring_rows(piece, way, step):
        half = halves[kinds[piece]]
        start = ring_block(way, step) * 2 * half
        if piece == 3:
            return aligned(start + side * half + way * (half // 2), half // 2)
        return aligned(start + way * half, half)

    def ring_copy(piece, way, step):
        return remote(
            parts[kinds[piece]].at[ring_rows(piece, way, step), spans[piece]],
            rings[piece].at[way, step],
            ring_send.at[piece, way, step], ring_recv.at[piece, way, step],
            (section, above if way == 0 else below),
        )

    def pair_copy(piece):
        half = halves[kinds[piece]]
        start = layer * 2 * half + (1 - side) * half
        return remote(
            parts[kinds[piece]].at[aligned(start, half), spans[piece]], pairs[piece],
            pair_send.at[piece], pair_recv.at[piece], (section, beside),
        )

    def early_copy(block):
        half = halves[1]
        start = block * 2 * half + (1 - side) * half
        return remote(
            part_down.at[aligned(start, half), spans[3]], pair_d.at[block],
            pair_send.at[3 + block], pair_recv.at[3 + block], (section, beside),
        )

    def final_rows(kind, which):
        half = halves[kind]
        quarter = half // 2
        return aligned(layer * 2 * half + side * half + which * quarter, quarter)

    def give_copies(piece):
        kind = kinds[piece]
        cols = spans[piece]
        return (
            remote(
                parts[kind].at[final_rows(kind, core), cols], fars[kind].at[0, :, cols],
                give_send.at[piece, 0], give_recv.at[piece, 0], (mirror, replica),
            ),
            remote(
                parts[kind].at[final_rows(kind, 1 - core), cols], fars[kind].at[1, :, cols],
                give_send.at[piece, 1], give_recv.at[piece, 1], (mirror, other),
            ),
            remote(
                parts[kind].at[final_rows(kind, 1 - core), cols], swaps[kind].at[:, cols],
                give_send.at[piece, 2], give_recv.at[piece, 2], (section, other),
            ),
        )

    state_copies = []
    for kind, (held_hbm, moment_hbm) in enumerate(
        ((up_hbm, moment_up_hbm), (down_hbm, moment_down_hbm))
    ):
        state_copies.append(
            pltpu.make_async_copy(moment_hbm.at[0], moments[kind], state_sem.at[kind, 0])
        )
        count = helds[kind].shape[1]
        for c in range(2):
            state_copies.append(
                pltpu.make_async_copy(
                    held_hbm.at[c, 0, aligned(replica * count, count), :],
                    helds[kind].at[c], state_sem.at[kind, 1 + c],
                )
            )

    w_up_copy.start()
    for slot in range(micro):
        own_copy(slot).start()
    w_down_copy.start()

    @pl.when(position > 0)
    def _():
        for copy in state_copies:
            copy.start()

    barrier = pltpu.get_barrier_semaphore()
    for device in (
        (after, replica), (before, replica), (section, other), (section, above),
        (section, below), (section, beside), (mirror, replica), (mirror, other),
    ):
        pl.semaphore_signal(barrier, inc=1, device_id=device, device_id_type=MESH)
    pl.semaphore_wait(barrier, 8)

    for slot in range(micro):
        swap_copy(slot).start()

    @pl.when(position == last)
    def _():
        for slot in range(micro):
            top_swap(slot).start()

    @pl.when(position == 0)
    def _():
        for slot in range(micro):
            top_own(slot).start()

    turned_down, turned_up = part_up, part_down
    across = min(256, model)

    def send_moments():
        for copy in state_copies:
            copy.wait()
        for kind in range(2):
            lows[kind][...] = moments[kind][...].astype(bf16)
            moment_copy(kind).start()

    w_up_copy.wait()

    @pl.loop(0, width // across)
    def _(t):
        cols = aligned(t * across, across)
        turned_up[cols, :] = w_up[:, cols].T

    w_down_copy.wait()

    @pl.loop(0, width // across)
    def _(t):
        cols = aligned(t * across, across)
        turned_down[:, cols] = w_down[cols, :].T

    @pl.when(position > 0)
    def _():
        send_moments()

    for slot in range(micro):
        own_copy(slot).wait()
        swap_copy(slot).wait()

    @pl.when(position == 0)
    def _():
        for copy in state_copies:
            copy.start()

    def forward(chunk):
        x = x_buf[2 * plan_ref[core, chunk // 2] + lax.rem(chunk, 2)]
        x_plan[chunk] = x

        for n in range(width // tile):
            cols = pl.ds(n * tile, tile)
            preact = jnp.dot(x, w_up[:, cols], preferred_element_type=f32)
            cdf = 0.5 * (1.0 + lax.erf(preact * root_half))
            hidden[chunk, :, cols] = (preact * cdf).astype(bf16)
            grown = cdf + preact * jnp.exp(-0.5 * preact * preact) * inv_root_tau
            slope[chunk, :, cols] = grown.astype(bf16)
        summed = x.astype(f32) + jnp.dot(hidden[chunk], w_down[...], preferred_element_type=f32)
        centre = summed - jnp.mean(summed, axis=-1, keepdims=True)
        scale_inv = lax.rsqrt(jnp.mean(centre * centre, axis=-1, keepdims=True) + norm_epsilon)
        normed[chunk] = centre * scale_inv
        scale_buf[chunk] = jnp.broadcast_to(scale_inv, (rows, 128))

    def backward(chunk):
        pltpu.make_async_copy(sent.at[chunk], e_buf.at[chunk], e_recv.at[chunk]).wait()
        upstream = e_buf[chunk].astype(f32)
        y = normed[chunk]
        scale_inv = scale_buf[chunk][:, :1]
        grad_sum = scale_inv * (
            upstream
            - jnp.mean(upstream, axis=-1, keepdims=True)
            - y * jnp.mean(upstream * y, axis=-1, keepdims=True)
        )
        low = grad_sum.astype(bf16)
        place = aligned(chunk * rows, rows)
        grad_low[place, :] = low
        for n in range(width // tile):
            cols = pl.ds(n * tile, tile)
            grad = jnp.dot(low, turned_down[:, cols], preferred_element_type=f32)
            grad = grad * slope[chunk, :, cols].astype(f32)
            grad_pre[place, cols] = grad.astype(bf16)

        @pl.when(position < last)
        def _():
            grad_in = jnp.dot(grad_pre[place, :], turned_up[...], preferred_element_type=f32)
            sent[chunk] = (grad_sum + grad_in).astype(bf16)
            relay_copy(chunk).start()

    lead = jnp.minimum(chunks, ahead * position)

    @pl.loop(0, 2 * chunks)
    def _(step):
        @pl.when(step < chunks)
        def _():
            forward(step)

        back = step - lead

        @pl.when(jnp.logical_and(back >= 0, back < chunks))
        def _():
            backward(back)

    total = chunks * rows
    up_rows, down_rows = 2 * halves[0], halves[1]

    def up_block(block):
        cols = aligned(block * up_rows, up_rows)
        left = x_plan[:, :, cols].reshape(total, up_rows)
        part_up[cols, :] = contract_rows(left, grad_pre[...]).astype(bf16)

    def down_block(block, which):
        cols = aligned(block * 2 * down_rows + which * down_rows, down_rows)
        left = hidden[:, :, cols].reshape(total, down_rows)
        part_down[cols, :] = contract_rows(left, grad_low[...]).astype(bf16)

    def add_rows(piece, place, value):
        part = parts[kinds[piece]]
        cols = spans[piece]
        part[place, cols] = (part[place, cols].astype(f32) + value.astype(f32)).astype(bf16)

    def turn(piece, step):
        for way in range(2):
            ring_copy(piece, way, step).wait_recv()
            add_rows(piece, ring_rows(piece, way, step + 1), rings[piece][way, step])
            if step < layers - 2:
                ring_copy(piece, way, step + 1).start()

    def give(piece):
        for copy in give_copies(piece):
            copy.start()

    def settle(piece):
        half = halves[kinds[piece]]
        pair_copy(piece).wait_recv()
        add_rows(piece, aligned(layer * 2 * half + side * half, half), pairs[piece][...])
        give(piece)

    def update(kind, out, out_moment):
        for piece in (2 * kind, 2 * kind + 1):
            for copy in give_copies(piece):
                copy.wait_recv()
        own = parts[kind][final_rows(kind, core), :].astype(f32)
        got = swaps[kind][...].astype(f32)
        same = fars[kind][0].astype(f32)
        cross = fars[kind][1].astype(f32)
        zero = core == 0
        grad = jnp.where(zero, own + cross, got + same)
        grad_mirror = jnp.where(zero, got + same, own + cross)
        moment = momentum_decay * moments[kind][...] + grad
        out_moment[...] = moment
        out[0] = (helds[kind][0].astype(f32) - step_size * moment).astype(bf16)
        mirrored = momentum_decay * theirs[kind][...].astype(f32) + grad_mirror
        out[1] = (helds[kind][1].astype(f32) - step_size * mirrored).astype(bf16)

    order = (layers - 1, 1, 2, 0)

    @pl.loop(0, 2)
    def _(i):
        up_block(lax.rem(layer + jnp.where(i == 0, order[0], order[1]), layers))

        @pl.when(i == 0)
        def _():
            ring_copy(0, 0, 0).start()
            ring_copy(1, 0, 0).start()

        @pl.when(i == 1)
        def _():
            ring_copy(0, 1, 0).start()
            ring_copy(1, 1, 0).start()

    def place(shift):
        return lax.rem(layer + shift, layers)

    def down_early(shift):
        down_block(place(shift), 1 - side)
        early_copy(place(shift)).start()

    @pl.loop(0, 2)
    def _(i):
        down_early(jnp.where(i == 0, order[0], order[1]))

    up_block(place(order[2]))
    down_early(order[2])
    turn(0, 0)
    turn(1, 0)
    down_early(order[3])
    up_block(place(order[3]))

    @pl.loop(0, 2)
    def _(i):
        down_block(place(jnp.where(i == 0, order[0], order[1])), side)

    turn(0, 1)
    turn(1, 1)
    for way in range(2):
        ring_copy(2, way, 0).start()

    @pl.loop(0, 2)
    def _(i):
        down_block(place(jnp.where(i == 0, order[2], order[3])), side)

    turn(0, 2)
    pair_copy(0).start()
    turn(1, 2)
    pair_copy(1).start()

    @pl.loop(0, layers)
    def _(block):
        early_copy(block).wait_recv()
        add_rows(3, aligned(block * 2 * down_rows + side * down_rows, down_rows), pair_d[block])

    for way in range(2):
        ring_copy(3, way, 0).start()
    settle(0)
    turn(2, 0)
    settle(1)
    turn(3, 0)
    turn(2, 1)
    turn(3, 1)
    turn(2, 2)
    pair_copy(2).start()
    turn(3, 2)
    give(3)

    @pl.when(position == 0)
    def _():
        send_moments()

    settle(2)
    for kind in range(2):
        moment_copy(kind).wait()
    update(0, new_up, new_moment_up)
    update(1, new_down, new_moment_down)

    for piece in range(4):
        for way in range(2):
            for step in range(layers - 1):
                ring_copy(piece, way, step).wait_send()
        for copy in give_copies(piece):
            copy.wait_send()
    for piece in range(3):
        pair_copy(piece).wait_send()
    for block in range(layers):
        early_copy(block).wait_send()

    @pl.when(position < last)
    def _():
        for chunk in range(chunks):
            relay_copy(chunk).wait_send()

    @pl.when(position == last)
    def _():
        for slot in range(micro):
            top_swap(slot).wait_send()


def relay(sections, replicas, plan, inputs, top_grad, up_weight, down_weight, up_moment, down_moment):
    micro, rows, model = inputs.shape[2:]
    width = up_weight.shape[3]
    chunks = 2 * micro
    total = chunks * rows
    layers = replicas // 4
    half_up, half_down = model // (2 * layers), width // (2 * layers)
    held_up, held_down = half_up // 2, half_down // 2
    cut = model * 3 // 8
    dma = pltpu.SemaphoreType.DMA
    flops = 2 * 6 * total * model * width
    return pl.pallas_call(
        functools.partial(
            relay_kernel, sections, replicas, micro, rows, model, width, min(512, width), 3
        ),
        out_shape=[
            jax.ShapeDtypeStruct((2, held_up, width), bf16),
            jax.ShapeDtypeStruct((2, held_down, model), bf16),
            jax.ShapeDtypeStruct((held_up, width), f32),
            jax.ShapeDtypeStruct((held_down, model), f32),
        ],
        in_specs=[pl.BlockSpec(memory_space=pltpu.SMEM)] + [pl.BlockSpec(memory_space=pl.ANY)] * 6,
        out_specs=[pl.BlockSpec(memory_space=pltpu.VMEM)] * 4,
        scratch_shapes=[
            pltpu.VMEM((model, width), bf16),
            pltpu.VMEM((width, model), bf16),
            pltpu.VMEM((chunks, rows, model), bf16),
            pltpu.VMEM((chunks, rows, model), bf16),
            pltpu.VMEM((chunks, rows, width), bf16),
            pltpu.VMEM((chunks, rows, width), bf16),
            pltpu.VMEM((chunks, rows, model), f32),
            pltpu.VMEM((chunks, rows, 128), f32),
            pltpu.VMEM((total, width), bf16),
            pltpu.VMEM((total, model), bf16),
            pltpu.VMEM((chunks, rows, model), bf16),
            pltpu.VMEM((chunks, rows, model), bf16),
            pltpu.VMEM((model, width), bf16),
            pltpu.VMEM((width, model), bf16),
            pltpu.VMEM((2, 2, layers - 1, half_up, width // 2), bf16),
            pltpu.VMEM((2, layers - 1, half_down, cut), bf16),
            pltpu.VMEM((2, layers - 1, half_down // 2, model - cut), bf16),
            pltpu.VMEM((2, half_up, width // 2), bf16),
            pltpu.VMEM((half_down, cut), bf16),
            pltpu.VMEM((layers, half_down, model - cut), bf16),
            pltpu.VMEM((held_up, width), bf16),
            pltpu.VMEM((held_down, model), bf16),
            pltpu.VMEM((2, held_up, width), bf16),
            pltpu.VMEM((2, held_down, model), bf16),
            pltpu.VMEM((held_up, width), f32),
            pltpu.VMEM((held_down, model), f32),
            pltpu.VMEM((held_up, width), bf16),
            pltpu.VMEM((held_down, model), bf16),
            pltpu.VMEM((held_up, width), bf16),
            pltpu.VMEM((held_down, model), bf16),
            pltpu.VMEM((2, held_up, width), bf16),
            pltpu.VMEM((2, held_down, model), bf16),
            dma((2,)),
            dma((micro,)),
            dma((micro,)),
            dma((micro,)),
            dma((micro,)),
            dma((chunks,)),
            dma((chunks,)),
            dma((2, 3)),
            dma((2,)),
            dma((2,)),
            dma((4, 2, layers - 1)),
            dma((4, 2, layers - 1)),
            dma((3 + layers,)),
            dma((3 + layers,)),
            dma((4, 3)),
            dma((4, 3)),
        ],
        compiler_params=pltpu.CompilerParams(
            collective_id=0, has_side_effects=True, vmem_limit_bytes=60 * 1024 * 1024
        ),
        cost_estimate=pl.CostEstimate(flops=flops, bytes_accessed=24 << 20, transcendentals=0),
    )(plan, inputs, top_grad, up_weight, down_weight, up_moment, down_moment)


def hand_on_kernel(count, *refs):
    sources, targets = refs[:count], refs[count:2 * count]
    staged, load_sem, store_sem = refs[2 * count:3 * count], refs[3 * count], refs[3 * count + 1]
    loads = []
    stores = []
    for i in range(count):
        half = sources[i].shape[0] // 2
        for j in range(2):
            rows = pl.ds(j * half, half)
            loads.append(pltpu.make_async_copy(
                sources[i].at[rows], staged[i].at[rows], load_sem.at[i, j]
            ))
            stores.append(pltpu.make_async_copy(
                staged[i].at[rows], targets[i].at[rows], store_sem.at[i, j]
            ))
    for load in loads:
        load.start()
    for load, store in zip(loads, stores):
        load.wait()
        store.start()
    for store in stores:
        store.wait()


def hand_on(*values):
    count = len(values)
    return pl.pallas_call(
        functools.partial(hand_on_kernel, count),
        out_shape=[jax.ShapeDtypeStruct(v.shape, v.dtype) for v in values],
        in_specs=[pl.BlockSpec(memory_space=pl.ANY)] * count,
        out_specs=[pl.BlockSpec(memory_space=pl.ANY)] * count,
        scratch_shapes=[pltpu.VMEM(v.shape, v.dtype) for v in values]
        + [pltpu.SemaphoreType.DMA((count, 2))] * 2,
        compiler_params=pltpu.CompilerParams(vmem_limit_bytes=60 * 1024 * 1024),
    )(*values)


def on_device(section_inputs, top_grad, plan, up_weight, down_weight, up_moment, down_moment):
    new_up, new_down, moment_up, moment_down = hand_on(*relay(
        lax.axis_size("section"), lax.axis_size("dp"), plan, section_inputs,
        top_grad, up_weight, down_weight, up_moment, down_moment,
    ))
    return (new_up[:, None], new_down[:, None], moment_up[None], moment_down[None])


def solution(mesh):
    in_specs = (
        P(None, "section", None, "dp", None),
        P(None, None, "dp", None),
        P(),
        P(None, "section", None, None),
        P(None, "section", None, None),
        P("section", "dp", None),
        P("section", "dp", None),
    )
    out_specs = (
        P(None, "section", "dp", None),
        P(None, "section", "dp", None),
        P("section", "dp", None),
        P("section", "dp", None),
    )
    return jax.shard_map(
        on_device, mesh=mesh, in_specs=in_specs, out_specs=out_specs, check_vma=False
    )
```

```python
import functools

import jax
import jax.numpy as jnp
from jax import lax
from jax.experimental import pallas as pl
from jax.experimental.pallas import tpu as pltpu
from jax.sharding import PartitionSpec as P

norm_epsilon = 1e-06
momentum_decay = 0.9
step_size = 0.01
root_half = 0.7071067811865476
inv_root_tau = 0.3989422804014327
MESH = pl.DeviceIdType.MESH
bf16 = jnp.bfloat16
f32 = jnp.float32


def contract_rows(left, right):
    return lax.dot_general(
        left, right, (((0,), (0,)), ((), ())), preferred_element_type=f32
    )


def relay_kernel(
    sections, replicas, micro, rows, model, width, tile, ahead,
    plan_ref, inputs_hbm, top_hbm, up_hbm, down_hbm, moment_up_hbm, moment_down_hbm,
    new_up, new_down, new_moment_up, new_moment_down,
    w_up, w_down, x_buf, x_plan, hidden, slope, normed, scale_buf, grad_pre, grad_low, e_buf, sent,
    part_up, part_down, ring_up, ring_c, ring_d, pair_up, pair_c, pair_d, swap_up, swap_down,
    far_up, far_down, moment_up, moment_down, low_up, low_down, their_up, their_down,
    held_up, held_down,
    w_sem, own_sem, swap_send, swap_recv, top_send, e_recv, e_send,
    state_sem, moment_send, moment_recv, ring_send, ring_recv, pair_send, pair_recv,
    give_send, give_recv,
):
    section = lax.axis_index("section")
    replica = lax.axis_index("dp")
    core = lax.rem(replica, 2)
    other = replica + 1 - 2 * core
    side = lax.rem(replica // 2, 2)
    layer = replica // 4
    layers = replicas // 4
    above = lax.rem(replica + 4, replicas)
    below = lax.rem(replica + replicas - 4, replicas)
    beside = replica + 2 - 4 * side
    mirror = sections - 1 - section
    position = jnp.where(core == 0, sections - 1 - section, section)
    step_to = 2 * core - 1
    after = lax.rem(section + step_to + sections, sections)
    before = lax.rem(section - step_to + sections, sections)
    chunks = 2 * micro
    last = sections - 1
    parts = (part_up, part_down)
    rings = (ring_up.at[0], ring_up.at[1], ring_c, ring_d)
    pairs = (pair_up.at[0], pair_up.at[1], pair_c)
    kinds = (0, 0, 1, 1)
    cut = ring_c.shape[-1]
    spans = (
        pl.ds(0, width // 2), pl.ds(width // 2, width // 2),
        pl.ds(0, cut), pl.ds(cut, model - cut),
    )
    swaps = (swap_up, swap_down)
    fars = (far_up, far_down)
    lows = (low_up, low_down)
    theirs = (their_up, their_down)
    moments = (moment_up, moment_down)
    helds = (held_up, held_down)
    halves = (model // (2 * layers), width // (2 * layers))

    w_up_copy = pltpu.make_async_copy(up_hbm.at[core, 0], w_up, w_sem.at[0])
    w_down_copy = pltpu.make_async_copy(down_hbm.at[core, 0], w_down, w_sem.at[1])

    def aligned(start, size):
        return pl.ds(pl.multiple_of(start, size), size)

    def own_copy(slot):
        return pltpu.make_async_copy(
            inputs_hbm.at[core, 0, slot], x_buf.at[2 * slot + core], own_sem.at[slot]
        )

    def remote(src, dst, send, recv, device):
        return pltpu.make_async_remote_copy(
            src_ref=src, dst_ref=dst, send_sem=send, recv_sem=recv,
            device_id=device, device_id_type=MESH,
        )

    def swap_copy(slot):
        return remote(
            inputs_hbm.at[1 - core, 0, slot], x_buf.at[2 * slot + core],
            swap_send.at[slot], swap_recv.at[slot], (section, other),
        )

    def top_own(slot):
        return pltpu.make_async_copy(
            top_hbm.at[core, slot], e_buf.at[2 * slot + core], e_recv.at[2 * slot + core]
        )

    def top_swap(slot):
        return remote(
            top_hbm.at[1 - core, slot], e_buf.at[2 * slot + core],
            top_send.at[slot], e_recv.at[2 * slot + core], (section, other),
        )

    def relay_copy(chunk):
        return remote(
            sent.at[chunk], e_buf.at[chunk], e_send.at[chunk], e_recv.at[chunk], (after, replica)
        )

    def moment_copy(kind):
        return remote(
            lows[kind], theirs[kind], moment_send.at[kind], moment_recv.at[kind], (mirror, replica)
        )

    def ring_block(way, step):
        shift = layers - 1 - step if way == 0 else 1 + step
        return lax.rem(layer + shift, layers)

    def ring_rows(piece, way, step):
        half = halves[kinds[piece]]
        start = ring_block(way, step) * 2 * half
        if piece == 3:
            return aligned(start + side * half + way * (half // 2), half // 2)
        return aligned(start + way * half, half)

    def ring_copy(piece, way, step):
        return remote(
            parts[kinds[piece]].at[ring_rows(piece, way, step), spans[piece]],
            rings[piece].at[way, step],
            ring_send.at[piece, way, step], ring_recv.at[piece, way, step],
            (section, above if way == 0 else below),
        )

    def pair_copy(piece):
        half = halves[kinds[piece]]
        start = layer * 2 * half + (1 - side) * half
        return remote(
            parts[kinds[piece]].at[aligned(start, half), spans[piece]], pairs[piece],
            pair_send.at[piece], pair_recv.at[piece], (section, beside),
        )

    def early_copy(block):
        half = halves[1]
        start = block * 2 * half + (1 - side) * half
        return remote(
            part_down.at[aligned(start, half), spans[3]], pair_d.at[block],
            pair_send.at[3 + block], pair_recv.at[3 + block], (section, beside),
        )

    def final_rows(kind, which):
        half = halves[kind]
        quarter = half // 2
        return aligned(layer * 2 * half + side * half + which * quarter, quarter)

    def give_copies(piece):
        kind = kinds[piece]
        cols = spans[piece]
        return (
            remote(
                parts[kind].at[final_rows(kind, core), cols], fars[kind].at[0, :, cols],
                give_send.at[piece, 0], give_recv.at[piece, 0], (mirror, replica),
            ),
            remote(
                parts[kind].at[final_rows(kind, 1 - core), cols], fars[kind].at[1, :, cols],
                give_send.at[piece, 1], give_recv.at[piece, 1], (mirror, other),
            ),
            remote(
                parts[kind].at[final_rows(kind, 1 - core), cols], swaps[kind].at[:, cols],
                give_send.at[piece, 2], give_recv.at[piece, 2], (section, other),
            ),
        )

    state_copies = []
    for kind, (held_hbm, moment_hbm) in enumerate(
        ((up_hbm, moment_up_hbm), (down_hbm, moment_down_hbm))
    ):
        state_copies.append(
            pltpu.make_async_copy(moment_hbm.at[0], moments[kind], state_sem.at[kind, 0])
        )
        count = helds[kind].shape[1]
        for c in range(2):
            state_copies.append(
                pltpu.make_async_copy(
                    held_hbm.at[c, 0, aligned(replica * count, count), :],
                    helds[kind].at[c], state_sem.at[kind, 1 + c],
                )
            )

    w_up_copy.start()
    for slot in range(micro):
        own_copy(slot).start()
    w_down_copy.start()

    @pl.when(position > 0)
    def _():
        for copy in state_copies:
            copy.start()

    barrier = pltpu.get_barrier_semaphore()
    for device in (
        (after, replica), (before, replica), (section, other), (section, above),
        (section, below), (section, beside), (mirror, replica), (mirror, other),
    ):
        pl.semaphore_signal(barrier, inc=1, device_id=device, device_id_type=MESH)
    pl.semaphore_wait(barrier, 8)

    for slot in range(micro):
        swap_copy(slot).start()

    @pl.when(position == last)
    def _():
        for slot in range(micro):
            top_swap(slot).start()

    @pl.when(position == 0)
    def _():
        for slot in range(micro):
            top_own(slot).start()

    turned_down, turned_up = part_up, part_down
    across = min(256, model)

    def send_moments():
        for copy in state_copies:
            copy.wait()
        for kind in range(2):
            lows[kind][...] = moments[kind][...].astype(bf16)
            moment_copy(kind).start()

    w_up_copy.wait()

    @pl.loop(0, width // across)
    def _(t):
        cols = aligned(t * across, across)
        turned_up[cols, :] = w_up[:, cols].T

    w_down_copy.wait()

    @pl.loop(0, width // across)
    def _(t):
        cols = aligned(t * across, across)
        turned_down[:, cols] = w_down[cols, :].T

    @pl.when(position > 0)
    def _():
        send_moments()

    for slot in range(micro):
        own_copy(slot).wait()
        swap_copy(slot).wait()

    @pl.when(position == 0)
    def _():
        for copy in state_copies:
            copy.start()

    def forward(chunk):
        x = x_buf[2 * plan_ref[core, chunk // 2] + lax.rem(chunk, 2)]
        x_plan[chunk] = x

        for n in range(width // tile):
            cols = pl.ds(n * tile, tile)
            preact = jnp.dot(x, w_up[:, cols], preferred_element_type=f32)
            cdf = 0.5 * (1.0 + lax.erf(preact * root_half))
            hidden[chunk, :, cols] = (preact * cdf).astype(bf16)
            grown = cdf + preact * jnp.exp(-0.5 * preact * preact) * inv_root_tau
            slope[chunk, :, cols] = grown.astype(bf16)
        summed = x.astype(f32) + jnp.dot(hidden[chunk], w_down[...], preferred_element_type=f32)
        centre = summed - jnp.mean(summed, axis=-1, keepdims=True)
        scale_inv = lax.rsqrt(jnp.mean(centre * centre, axis=-1, keepdims=True) + norm_epsilon)
        normed[chunk] = centre * scale_inv
        scale_buf[chunk] = jnp.broadcast_to(scale_inv, (rows, 128))

    def backward(chunk):
        pltpu.make_async_copy(sent.at[chunk], e_buf.at[chunk], e_recv.at[chunk]).wait()
        upstream = e_buf[chunk].astype(f32)
        y = normed[chunk]
        scale_inv = scale_buf[chunk][:, :1]
        grad_sum = scale_inv * (
            upstream
            - jnp.mean(upstream, axis=-1, keepdims=True)
            - y * jnp.mean(upstream * y, axis=-1, keepdims=True)
        )
        low = grad_sum.astype(bf16)
        place = aligned(chunk * rows, rows)
        grad_low[place, :] = low
        for n in range(width // tile):
            cols = pl.ds(n * tile, tile)
            grad = jnp.dot(low, turned_down[:, cols], preferred_element_type=f32)
            grad = grad * slope[chunk, :, cols].astype(f32)
            grad_pre[place, cols] = grad.astype(bf16)

        @pl.when(position < last)
        def _():
            grad_in = jnp.dot(grad_pre[place, :], turned_up[...], preferred_element_type=f32)
            sent[chunk] = (grad_sum + grad_in).astype(bf16)
            relay_copy(chunk).start()

    lead = jnp.minimum(chunks, ahead * position)

    @pl.loop(0, 2 * chunks)
    def _(step):
        @pl.when(step < chunks)
        def _():
            forward(step)

        back = step - lead

        @pl.when(jnp.logical_and(back >= 0, back < chunks))
        def _():
            backward(back)

    total = chunks * rows
    up_rows, down_rows = 2 * halves[0], halves[1]

    def up_block(block):
        cols = aligned(block * up_rows, up_rows)
        left = x_plan[:, :, cols].reshape(total, up_rows)
        part_up[cols, :] = contract_rows(left, grad_pre[...]).astype(bf16)

    def down_block(block, which):
        cols = aligned(block * 2 * down_rows + which * down_rows, down_rows)
        left = hidden[:, :, cols].reshape(total, down_rows)
        part_down[cols, :] = contract_rows(left, grad_low[...]).astype(bf16)

    def add_rows(piece, place, value):
        part = parts[kinds[piece]]
        cols = spans[piece]
        part[place, cols] = (part[place, cols].astype(f32) + value.astype(f32)).astype(bf16)

    def turn(piece, step):
        for way in range(2):
            ring_copy(piece, way, step).wait_recv()
            add_rows(piece, ring_rows(piece, way, step + 1), rings[piece][way, step])
            if step < layers - 2:
                ring_copy(piece, way, step + 1).start()

    def give(piece):
        for copy in give_copies(piece):
            copy.start()

    def settle(piece):
        half = halves[kinds[piece]]
        pair_copy(piece).wait_recv()
        add_rows(piece, aligned(layer * 2 * half + side * half, half), pairs[piece][...])
        give(piece)

    def update(kind, out, out_moment):
        for piece in (2 * kind, 2 * kind + 1):
            for copy in give_copies(piece):
                copy.wait_recv()
        own = parts[kind][final_rows(kind, core), :].astype(f32)
        got = swaps[kind][...].astype(f32)
        same = fars[kind][0].astype(f32)
        cross = fars[kind][1].astype(f32)
        zero = core == 0
        grad = jnp.where(zero, own + cross, got + same)
        grad_mirror = jnp.where(zero, got + same, own + cross)
        moment = momentum_decay * moments[kind][...] + grad
        out_moment[...] = moment
        out[0] = (helds[kind][0].astype(f32) - step_size * moment).astype(bf16)
        mirrored = momentum_decay * theirs[kind][...].astype(f32) + grad_mirror
        out[1] = (helds[kind][1].astype(f32) - step_size * mirrored).astype(bf16)

    order = (layers - 1, 1, 2, 0)

    @pl.loop(0, 2)
    def _(i):
        up_block(lax.rem(layer + jnp.where(i == 0, order[0], order[1]), layers))

        @pl.when(i == 0)
        def _():
            ring_copy(0, 0, 0).start()
            ring_copy(1, 0, 0).start()

        @pl.when(i == 1)
        def _():
            ring_copy(0, 1, 0).start()
            ring_copy(1, 1, 0).start()

    def place(shift):
        return lax.rem(layer + shift, layers)

    def down_early(shift):
        down_block(place(shift), 1 - side)
        early_copy(place(shift)).start()

    @pl.loop(0, 2)
    def _(i):
        down_early(jnp.where(i == 0, order[0], order[1]))

    up_block(place(order[2]))
    down_early(order[2])
    turn(0, 0)
    turn(1, 0)
    down_early(order[3])
    up_block(place(order[3]))

    @pl.loop(0, 2)
    def _(i):
        down_block(place(jnp.where(i == 0, order[0], order[1])), side)

    turn(0, 1)
    turn(1, 1)
    for way in range(2):
        ring_copy(2, way, 0).start()

    @pl.loop(0, 2)
    def _(i):
        down_block(place(jnp.where(i == 0, order[2], order[3])), side)

    turn(0, 2)
    pair_copy(0).start()
    turn(1, 2)
    pair_copy(1).start()

    @pl.loop(0, layers)
    def _(block):
        early_copy(block).wait_recv()
        add_rows(3, aligned(block * 2 * down_rows + side * down_rows, down_rows), pair_d[block])

    for way in range(2):
        ring_copy(3, way, 0).start()
    turn(2, 0)
    settle(0)
    turn(3, 0)
    settle(1)
    turn(2, 1)
    turn(3, 1)
    turn(2, 2)
    pair_copy(2).start()
    turn(3, 2)
    give(3)

    @pl.when(position == 0)
    def _():
        send_moments()

    settle(2)
    for kind in range(2):
        moment_copy(kind).wait()
    update(0, new_up, new_moment_up)
    update(1, new_down, new_moment_down)

    for piece in range(4):
        for way in range(2):
            for step in range(layers - 1):
                ring_copy(piece, way, step).wait_send()
        for copy in give_copies(piece):
            copy.wait_send()
    for piece in range(3):
        pair_copy(piece).wait_send()
    for block in range(layers):
        early_copy(block).wait_send()

    @pl.when(position < last)
    def _():
        for chunk in range(chunks):
            relay_copy(chunk).wait_send()

    @pl.when(position == last)
    def _():
        for slot in range(micro):
            top_swap(slot).wait_send()


def relay(sections, replicas, plan, inputs, top_grad, up_weight, down_weight, up_moment, down_moment):
    micro, rows, model = inputs.shape[2:]
    width = up_weight.shape[3]
    chunks = 2 * micro
    total = chunks * rows
    layers = replicas // 4
    half_up, half_down = model // (2 * layers), width // (2 * layers)
    held_up, held_down = half_up // 2, half_down // 2
    cut = model * 3 // 8
    dma = pltpu.SemaphoreType.DMA
    flops = 2 * 6 * total * model * width
    return pl.pallas_call(
        functools.partial(
            relay_kernel, sections, replicas, micro, rows, model, width, min(512, width), 3
        ),
        out_shape=[
            jax.ShapeDtypeStruct((2, held_up, width), bf16),
            jax.ShapeDtypeStruct((2, held_down, model), bf16),
            jax.ShapeDtypeStruct((held_up, width), f32),
            jax.ShapeDtypeStruct((held_down, model), f32),
        ],
        in_specs=[pl.BlockSpec(memory_space=pltpu.SMEM)] + [pl.BlockSpec(memory_space=pl.ANY)] * 6,
        out_specs=[pl.BlockSpec(memory_space=pltpu.VMEM)] * 4,
        scratch_shapes=[
            pltpu.VMEM((model, width), bf16),
            pltpu.VMEM((width, model), bf16),
            pltpu.VMEM((chunks, rows, model), bf16),
            pltpu.VMEM((chunks, rows, model), bf16),
            pltpu.VMEM((chunks, rows, width), bf16),
            pltpu.VMEM((chunks, rows, width), bf16),
            pltpu.VMEM((chunks, rows, model), f32),
            pltpu.VMEM((chunks, rows, 128), f32),
            pltpu.VMEM((total, width), bf16),
            pltpu.VMEM((total, model), bf16),
            pltpu.VMEM((chunks, rows, model), bf16),
            pltpu.VMEM((chunks, rows, model), bf16),
            pltpu.VMEM((model, width), bf16),
            pltpu.VMEM((width, model), bf16),
            pltpu.VMEM((2, 2, layers - 1, half_up, width // 2), bf16),
            pltpu.VMEM((2, layers - 1, half_down, cut), bf16),
            pltpu.VMEM((2, layers - 1, half_down // 2, model - cut), bf16),
            pltpu.VMEM((2, half_up, width // 2), bf16),
            pltpu.VMEM((half_down, cut), bf16),
            pltpu.VMEM((layers, half_down, model - cut), bf16),
            pltpu.VMEM((held_up, width), bf16),
            pltpu.VMEM((held_down, model), bf16),
            pltpu.VMEM((2, held_up, width), bf16),
            pltpu.VMEM((2, held_down, model), bf16),
            pltpu.VMEM((held_up, width), f32),
            pltpu.VMEM((held_down, model), f32),
            pltpu.VMEM((held_up, width), bf16),
            pltpu.VMEM((held_down, model), bf16),
            pltpu.VMEM((held_up, width), bf16),
            pltpu.VMEM((held_down, model), bf16),
            pltpu.VMEM((2, held_up, width), bf16),
            pltpu.VMEM((2, held_down, model), bf16),
            dma((2,)),
            dma((micro,)),
            dma((micro,)),
            dma((micro,)),
            dma((micro,)),
            dma((chunks,)),
            dma((chunks,)),
            dma((2, 3)),
            dma((2,)),
            dma((2,)),
            dma((4, 2, layers - 1)),
            dma((4, 2, layers - 1)),
            dma((3 + layers,)),
            dma((3 + layers,)),
            dma((4, 3)),
            dma((4, 3)),
        ],
        compiler_params=pltpu.CompilerParams(
            collective_id=0, has_side_effects=True, vmem_limit_bytes=60 * 1024 * 1024
        ),
        cost_estimate=pl.CostEstimate(flops=flops, bytes_accessed=24 << 20, transcendentals=0),
    )(plan, inputs, top_grad, up_weight, down_weight, up_moment, down_moment)


def hand_on_kernel(count, *refs):
    sources, targets = refs[:count], refs[count:2 * count]
    staged, load_sem, store_sem = refs[2 * count:3 * count], refs[3 * count], refs[3 * count + 1]
    loads = []
    stores = []
    for i in range(count):
        half = sources[i].shape[0] // 2
        for j in range(2):
            rows = pl.ds(j * half, half)
            loads.append(pltpu.make_async_copy(
                sources[i].at[rows], staged[i].at[rows], load_sem.at[i, j]
            ))
            stores.append(pltpu.make_async_copy(
                staged[i].at[rows], targets[i].at[rows], store_sem.at[i, j]
            ))
    for load in loads:
        load.start()
    for load, store in zip(loads, stores):
        load.wait()
        store.start()
    for store in stores:
        store.wait()


def hand_on(*values):
    count = len(values)
    return pl.pallas_call(
        functools.partial(hand_on_kernel, count),
        out_shape=[jax.ShapeDtypeStruct(v.shape, v.dtype) for v in values],
        in_specs=[pl.BlockSpec(memory_space=pl.ANY)] * count,
        out_specs=[pl.BlockSpec(memory_space=pl.ANY)] * count,
        scratch_shapes=[pltpu.VMEM(v.shape, v.dtype) for v in values]
        + [pltpu.SemaphoreType.DMA((count, 2))] * 2,
        compiler_params=pltpu.CompilerParams(vmem_limit_bytes=60 * 1024 * 1024),
    )(*values)


def on_device(section_inputs, top_grad, plan, up_weight, down_weight, up_moment, down_moment):
    new_up, new_down, moment_up, moment_down = hand_on(*relay(
        lax.axis_size("section"), lax.axis_size("dp"), plan, section_inputs,
        top_grad, up_weight, down_weight, up_moment, down_moment,
    ))
    return (new_up[:, None], new_down[:, None], moment_up[None], moment_down[None])


def solution(mesh):
    in_specs = (
        P(None, "section", None, "dp", None),
        P(None, None, "dp", None),
        P(),
        P(None, "section", None, None),
        P(None, "section", None, None),
        P("section", "dp", None),
        P("section", "dp", None),
    )
    out_specs = (
        P(None, "section", "dp", None),
        P(None, "section", "dp", None),
        P("section", "dp", None),
        P("section", "dp", None),
    )
    return jax.shard_map(
        on_device, mesh=mesh, in_specs=in_specs, out_specs=out_specs, check_vma=False
    )
```
